32 devices in a mesh: seq: 4 (over y, core), fsdp: 8 (over z, x).
Axes of the slice: x: 2, y: 2, z: 4, core: 2. Of those that a mesh axis runs over, the one named last changes fastest.
Arguments:
- tokens: bfloat16 [2, 16, 1024, 768], P(None, 'fsdp', 'seq'), may hold values from -6 to 6
- segment_ids: int32 [2, 16, 1024], P(None, 'fsdp', 'seq'), may hold values from 0 to 7, never falling along the last dimension, each value on 1 to 512 neighbouring positions
- out_cotangent: bfloat16 [2, 16, 1024, 768], P(None, 'fsdp', 'seq'), may hold values from -6 to 6
- query_weight: bfloat16 [768, 768], P('fsdp'), may hold values from -0.21875 to 0.21875
- query_bias: bfloat16 [768], P('fsdp'), may hold values from -3 to 3
- key_weight: bfloat16 [768, 768], P('fsdp'), may hold values from -0.21875 to 0.21875
- value_weight: bfloat16 [768, 768], P('fsdp'), may hold values from -0.21875 to 0.21875
- value_bias: bfloat16 [768], P('fsdp'), may hold values from -3 to 3
- output_weight: bfloat16 [768, 768], P('fsdp'), may hold values from -0.875 to 0.875
- output_bias: bfloat16 [768], P('fsdp'), may hold values from -3 to 3
- attn_gain: bfloat16 [768], P('fsdp'), may hold values from 0.099609375 to 1.8984375
- attn_shift: bfloat16 [768], P('fsdp'), may hold values from -3 to 3
- inner_weight: bfloat16 [768, 3072], P('fsdp'), may hold values from -0.21875 to 0.21875
- inner_bias: bfloat16 [3072], P('fsdp'), may hold values from -3 to 3
- outer_weight: bfloat16 [3072, 768], P('fsdp'), may hold values from -0.109375 to 0.109375
- outer_bias: bfloat16 [768], P('fsdp'), may hold values from -3 to 3
- final_gain: bfloat16 [768], P('fsdp'), may hold values from 0.099609375 to 1.8984375
- final_shift: bfloat16 [768], P('fsdp'), may hold values from -3 to 3
Outputs:
- layer_out: bfloat16 [2, 16, 1024, 768], P(None, 'fsdp', 'seq')
- input_grad: float32 [2, 16, 1024, 768], P(None, 'fsdp', 'seq')
- query_weight_grad: float32 [768, 768], P('fsdp')
- query_bias_grad: float32 [768], P('fsdp')
- key_weight_grad: float32 [768, 768], P('fsdp')
- value_weight_grad: float32 [768, 768], P('fsdp')
- value_bias_grad: float32 [768], P('fsdp')
- output_weight_grad: float32 [768, 768], P('fsdp')
- output_bias_grad: float32 [768], P('fsdp')
- attn_gain_grad: float32 [768], P('fsdp')
- attn_shift_grad: float32 [768], P('fsdp')
- inner_weight_grad: float32 [768, 3072], P('fsdp')
- inner_bias_grad: float32 [3072], P('fsdp')
- outer_weight_grad: float32 [3072, 768], P('fsdp')
- outer_bias_grad: float32 [768], P('fsdp')
- final_gain_grad: float32 [768], P('fsdp')
- final_shift_grad: float32 [768], P('fsdp')
The draws below stay inside these ranges and needn't reach their ends.
Inputs may be any that keep to these rules, and one draw needn't show every extreme that they name: `segment_ids`: along each sequence the document numbers never fall; every document spans 1 to 512 tokens, and one document of each sequence spans exactly 512.
All inputs are finite; a program needn't handle non-finite values.
Results may differ from the reference program's by a relative error of at most 0.014.
Values may be sent and summed in bfloat16 or wider, within the bound.
No kernel may reach another device: no remote copies, remote signals or barrier semaphores. Data moves between devices by JAX's collectives and lax.ppermute only.
A program may use at most 192 MiB of HBM per device.

```python
import math
import jax
import jax.numpy as jnp
import numpy as np
from jax import lax

D = 768
HEADS = 12
HEAD_DIM = 64
FF = 3072
LEN = 1024
MICRO = 2
DOCS = 8
NSEQ = 16


def block_levels(stream_key, shape, pieces, least, top_value):
    level = 1.0
    for dim, blocks in pieces:
        steps = jax.random.uniform(jax.random.fold_in(jax.random.fold_in(stream_key, 6), dim), (blocks,), jnp.float32, least / len(pieces), top_value / len(pieces))
        level = level * jnp.repeat(jnp.exp(steps), shape[dim] // blocks).reshape((-1,) + (1,) * (len(shape) - 1 - dim))
    return level


def length_profile(number_of, total, reach, skew):
    loads = [(1 << 20) // math.isqrt(standing ** skew) + 1 for standing in range(2, number_of + 1)]
    rest, counts = total - reach - (number_of - 1), [1] * (number_of - 1)
    while rest > 0:
        movable = [i for i in range(number_of - 1) if counts[i] < reach]
        pool, left = sum([loads[i] for i in movable]), rest
        for i in movable:
            extra = min(reach - counts[i], max(1, left * loads[i] // pool), rest)
            counts[i] = counts[i] + extra
            rest = rest - extra
    return np.array([reach] + counts)


def ragged_sizes(stream_key, amount, total, reach, slope):
    if amount == 2:
        one = jax.random.randint(stream_key, (), max(1, total - reach), min(reach, total - 1) + 1)
        return jnp.stack([one, total - one])
    lengths = jnp.asarray(length_profile(amount, total, reach, slope), jnp.int32)
    pairs = (amount - 1) // 2
    source_of, sink = lengths[1:1 + 2 * pairs:2], lengths[2:2 + 2 * pairs:2]
    room = jnp.minimum(source_of - 1, reach - sink)
    passed = jax.random.randint(jax.random.fold_in(stream_key, 1), (pairs,), 0, 1 << 20) % (room + 1)
    lengths = lengths.at[1:1 + 2 * pairs:2].set(source_of - passed).at[2:2 + 2 * pairs:2].set(sink + passed)
    return lengths[jax.random.permutation(jax.random.fold_in(stream_key, 2), amount)]


def gaussian(rng, extent, scale, bound, cuts=(), kind=jnp.bfloat16):
    factor_of = block_levels(rng, extent, cuts, -0.22, 0.18) if cuts else 1.0
    values = jax.random.normal(rng, extent, jnp.float32) * scale * factor_of
    return jnp.minimum(jnp.maximum(values, -bound), bound).astype(kind)


def setup_inputs(seed: int = 0) -> dict:
    key_of = jax.random.split(jax.random.key(seed), 19)
    tokens = gaussian(key_of[0], (MICRO, NSEQ, LEN, D), 1.0, 6.0, ((1, 8), (2, 4)))
    segment_ids = jax.vmap(lambda own: jnp.searchsorted(jnp.cumsum(ragged_sizes(own, DOCS, LEN, LEN // 2, 2)), jnp.arange(LEN), side="right"))(jax.random.split(key_of[1], MICRO * NSEQ)).reshape((MICRO, NSEQ, LEN)).astype(jnp.int32)
    out_cotangent = gaussian(key_of[2], (MICRO, NSEQ, LEN, D), 1.0, 6.0, ((1, 8), (2, 4)))
    query_weight = gaussian(key_of[3], (D, D), D ** -0.5, 0.21875, ((0, 8),))
    query_bias = gaussian(key_of[4], (D,), 0.5, 3.0, ((0, 8),))
    key_weight = gaussian(key_of[5], (D, D), D ** -0.5, 0.21875, ((0, 8),))
    value_weight = gaussian(key_of[6], (D, D), D ** -0.5, 0.21875, ((0, 8),))
    value_bias = gaussian(key_of[7], (D,), 0.5, 3.0, ((0, 8),))
    output_weight = gaussian(key_of[8], (D, D), (D // 16) ** -0.5, 0.875, ((0, 8),))
    output_bias = gaussian(key_of[9], (D,), 0.5, 3.0, ((0, 8),))
    attn_gain = jnp.clip(1.0 + 0.18 * jax.random.normal(key_of[10], (D,), jnp.float32), 0.099609375, 1.8984375).astype(jnp.bfloat16)
    attn_shift = gaussian(key_of[11], (D,), 0.5, 3.0, ((0, 8),))
    inner_weight = gaussian(key_of[12], (D, FF), D ** -0.5, 0.21875, ((0, 8),))
    inner_bias = gaussian(key_of[13], (FF,), 0.5, 3.0, ((0, 8),))
    outer_weight = gaussian(key_of[14], (FF, D), FF ** -0.5, 0.109375, ((0, 8),))
    outer_bias = gaussian(key_of[15], (D,), 0.5, 3.0, ((0, 8),))
    final_gain = jnp.clip(1.0 + 0.18 * jax.random.normal(key_of[16], (D,), jnp.float32), 0.099609375, 1.8984375).astype(jnp.bfloat16)
    final_shift = gaussian(key_of[17], (D,), 0.5, 3.0, ((0, 8),))
    return dict(tokens=tokens, segment_ids=segment_ids, out_cotangent=out_cotangent, query_weight=query_weight, query_bias=query_bias, key_weight=key_weight, value_weight=value_weight, value_bias=value_bias, output_weight=output_weight, output_bias=output_bias, attn_gain=attn_gain, attn_shift=attn_shift, inner_weight=inner_weight, inner_bias=inner_bias, outer_weight=outer_weight, outer_bias=outer_bias, final_gain=final_gain, final_shift=final_shift)


@jax.custom_vjp
def low(v):
    return lax.optimization_barrier(v.astype(jnp.bfloat16)).astype(jnp.float32)

@jax.custom_vjp
def low_back(v):
    return v

def low_keep(v):
    return (low(v), None)

def low_pass(kept, grad):
    return (grad,)

def back_keep(v):
    return (v, None)

def back_low(kept, grad):
    return (low(grad),)
low.defvjp(low_keep, low_pass)
low_back.defvjp(back_keep, back_low)
norm_eps = 1e-12
masked_fill = -1e+30

def matmul(left, right):
    return jnp.dot(left, right, precision=lax.Precision.HIGHEST, preferred_element_type=jnp.float32)

def layer_norm(values, gain, shift):
    center = values - lax.optimization_barrier(jnp.mean(values, axis=-1, keepdims=True))
    spread = lax.optimization_barrier(jnp.mean(center * center, axis=-1, keepdims=True))
    return center * lax.rsqrt(spread + norm_eps) * gain + shift

def attend_head(query_head, key_head, value_head, same_doc):
    raw = matmul(query_head, key_head.T) * (1.0 / math.sqrt(HEAD_DIM))
    scores = low_back(jnp.where(same_doc, raw, masked_fill))
    top = lax.optimization_barrier(jnp.max(scores, axis=-1, keepdims=True))
    expo = jnp.exp(scores - top)
    probs = expo / lax.optimization_barrier(jnp.sum(expo, axis=-1, keepdims=True))
    return matmul(low(probs), value_head)

def split_heads(values):
    return values.reshape(LEN, HEADS, HEAD_DIM).transpose(1, 0, 2)

def one_sequence(params, rows_in, doc_seq):
    query_mat, query_vec, key_mat, value_mat, value_vec, output_mat, output_vec, gain_first, shift_first, inner_mat, inner_vec, outer_mat, outer_vec, gain_final, shift_final = params
    queries = low(low_back(matmul(rows_in, query_mat) + query_vec))
    key_rows = low(low_back(matmul(rows_in, key_mat)))
    value_rows = low(low_back(matmul(rows_in, value_mat) + value_vec))
    same_doc = doc_seq[:, None] == doc_seq[None, :]
    attend_saved = jax.checkpoint(attend_head)

    def per_head(item):
        return attend_saved(item[0], item[1], item[2], same_doc)
    mixed = lax.map(per_head, (split_heads(queries), split_heads(key_rows), split_heads(value_rows)))
    attended = low(low_back(mixed.transpose(1, 0, 2).reshape(LEN, D)))
    branch = low_back(matmul(attended, output_mat) + output_vec)
    normed = layer_norm(rows_in + branch, gain_first, shift_first)
    inner = low_back(matmul(low(normed), inner_mat) + inner_vec)
    active = low(jax.nn.gelu(inner, approximate=False))
    branch_two = low_back(matmul(active, outer_mat) + outer_vec)
    return layer_norm(normed + branch_two, gain_final, shift_final)

def reference(tokens, segment_ids, out_cotangent, query_weight, query_bias, key_weight, value_weight, value_bias, output_weight, output_bias, attn_gain, attn_shift, inner_weight, inner_bias, outer_weight, outer_bias, final_gain, final_shift):
    params = tuple((piece.astype(jnp.float32) for piece in (query_weight, query_bias, key_weight, value_weight, value_bias, output_weight, output_bias, attn_gain, attn_shift, inner_weight, inner_bias, outer_weight, outer_bias, final_gain, final_shift)))
    rows_all = tokens.astype(jnp.float32).reshape(-1, LEN, D)
    docs_all = segment_ids.reshape(-1, LEN)
    cotangent = out_cotangent.astype(jnp.float32).reshape(-1, LEN, D)

    def forward(weights, inputs):

        def step(carry, item):
            return (carry, one_sequence(weights, item[0], item[1]))
        start = jnp.zeros((), jnp.float32)
        _, outputs = lax.scan(step, start, (inputs, docs_all))
        return outputs
    result, pull = jax.vjp(forward, params, rows_all)
    grads, input_grad = pull(cotangent)
    return (result.astype(jnp.bfloat16).reshape(tokens.shape), input_grad.reshape(tokens.shape), grads[0], grads[1], grads[2], grads[3], grads[4], grads[5], grads[6], grads[7], grads[8], grads[9], grads[10], grads[11], grads[12], grads[13], grads[14])
```

```python
import math

import jax
import jax.numpy as jnp
from jax import lax
from jax.experimental import pallas as pl
from jax.experimental.pallas import tpu as pltpu
from jax.sharding import PartitionSpec as P

F32=jnp.float32; BF=jnp.bfloat16
PAIR=128; HD=64; BIG=1e30

def dot_nn(a,b): return lax.dot_general(a,b,(((1,),(0,)),((),())),preferred_element_type=F32)
def dot_nt(a,b): return lax.dot_general(a,b,(((1,),(1,)),((),())),preferred_element_type=F32)
def dot_tn(a,b): return lax.dot_general(a,b,(((0,),(0,)),((),())),preferred_element_type=F32)

def split3(v):
    hi=v.astype(BF); r=v-hi.astype(F32); mid=r.astype(BF); lo=(r-mid.astype(F32)).astype(BF)
    return hi,mid,lo

def fwd_kernel(doc_ref,q_ref,k_ref,v_ref,o_ref,lse_ref,qa,ka,va):
    rows=q_ref.shape[0]
    lane=lax.broadcasted_iota(jnp.int32,(rows,PAIR),1)
    doc=doc_ref[...]
    for h in range(2):
        base=(1-h)*HD
        mine=(lane>=h*HD)&(lane<(h+1)*HD)
        same=(lane-base)==doc
        qa[...]=jnp.where(mine,q_ref[...]*jnp.asarray(0.125,BF),jnp.where(same,1.0,0.0).astype(BF))
        ka[...]=jnp.where(mine,k_ref[...],jnp.where(same|(lane<base)|(lane>=base+8),0.0,-BIG).astype(BF))
        va[...]=jnp.where(mine,v_ref[...],jnp.ones((),BF))
        bq=256
        for i in range(rows//bq):
            sl=slice(i*bq,(i+1)*bq)
            sc=dot_nt(qa[sl,:],ka[...])
            m=jnp.max(sc,axis=1,keepdims=True)
            p=jnp.exp(sc-m).astype(BF)
            o=dot_nn(p,va[...])
            l=o[:,base:base+1]
            lse_ref[sl,h:h+1]=m+jnp.log(l)
            out=(o/l).astype(BF)
            if h==0: o_ref[sl,:]=out
            else: o_ref[sl,:]=jnp.where(lane[sl,:]>=HD,out,o_ref[sl,:])

def attend(doc,qkv,interpret=False):
    rows=qkv.shape[0]; pairs=qkv.shape[1]//3//PAIR
    return pl.pallas_call(fwd_kernel,grid=(pairs,),
        in_specs=[pl.BlockSpec((rows,1),lambda h:(0,0))]+[pl.BlockSpec((rows,PAIR),lambda h,j=j:(0,h+j*pairs)) for j in range(3)],
        out_specs=[pl.BlockSpec((rows,PAIR),lambda h:(0,h)),pl.BlockSpec((None,rows,2),lambda h:(h,0,0))],
        out_shape=[jax.ShapeDtypeStruct((rows,pairs*PAIR),BF),jax.ShapeDtypeStruct((pairs,rows,2),F32)],
        scratch_shapes=[pltpu.VMEM((rows,PAIR),BF)]*3,
        compiler_params=pltpu.CompilerParams(vmem_limit_bytes=60<<20),
        cost_estimate=pl.CostEstimate(flops=4*rows*rows*PAIR*pairs*2,bytes_accessed=rows*PAIR*pairs*8,transcendentals=rows*rows*pairs*2),
        name="attend")(doc,qkv,qkv,qkv)

def bwd_kernel(doc_ref,q_ref,k_ref,v_ref,o_ref,do_ref,lse_ref,dq_ref,dk_ref,dv_ref,qa,ka,va,da,dqs):
    rows=q_ref.shape[0]
    lane=lax.broadcasted_iota(jnp.int32,(rows,PAIR),1)
    doc=doc_ref[...]
    dof=do_ref[...].astype(F32)*o_ref[...].astype(F32)
    for h in range(2):
        base=(1-h)*HD
        mine=(lane>=h*HD)&(lane<(h+1)*HD)
        rel=lane-base
        same=rel==doc
        delta=jnp.sum(jnp.where(mine,dof,0.0),axis=1,keepdims=True)
        lh,lm,ll=split3(-lse_ref[:,h:h+1]); dh,dm,dl=split3(-delta)
        one=jnp.ones((),BF); zero=jnp.zeros((),BF)
        aug_q=jnp.where(same,one,zero)
        aug_q=jnp.where(rel==8,lh,jnp.where(rel==9,lm,jnp.where(rel==10,ll,aug_q)))
        aug_k=jnp.where((rel>=0)&(rel<8)&(~same),jnp.asarray(-BIG,BF),zero)
        aug_k=jnp.where((rel>=8)&(rel<11),one,aug_k)
        aug_d=jnp.where(rel==8,dh,jnp.where(rel==9,dm,jnp.where(rel==10,dl,zero)))
        aug_v=jnp.where((rel>=8)&(rel<11),one,zero)
        qa[...]=jnp.where(mine,q_ref[...]*jnp.asarray(0.125,BF),aug_q)
        ka[...]=jnp.where(mine,k_ref[...],aug_k)
        va[...]=jnp.where(mine,v_ref[...],aug_v)
        da[...]=jnp.where(mine,do_ref[...],aug_d)
        bk=256
        for i in range(rows//bk):
            sl=slice(i*bk,(i+1)*bk)
            st=dot_nt(ka[sl,:],qa[...])
            pt=jnp.exp(st)
            dpt=dot_nt(va[sl,:],da[...])
            dst=(pt*dpt).astype(BF)
            dv=dot_nn(pt.astype(BF),da[...])
            dk=dot_nn(dst,qa[...])
            dq=dot_tn(dst,ka[sl,:])
            if i==0: dqs[...]=dq
            else: dqs[...]+=dq
            msl=mine[sl,:]
            if h==0:
                dv_ref[sl,:]=dv.astype(BF); dk_ref[sl,:]=dk.astype(BF)
            else:
                dv_ref[sl,:]=jnp.where(msl,dv.astype(BF),dv_ref[sl,:]); dk_ref[sl,:]=jnp.where(msl,dk.astype(BF),dk_ref[sl,:])
        dqv=(dqs[...]*0.125).astype(BF)
        if h==0: dq_ref[...]=dqv
        else: dq_ref[...]=jnp.where(mine,dqv,dq_ref[...])

def attend_back(doc,qkv,att,datt,lse,first=0,count=None):
    rows=qkv.shape[0]; pairs=qkv.shape[1]//3//PAIR
    n=count or pairs
    col=lambda h:(0,h+first)
    return pl.pallas_call(bwd_kernel,grid=(n,),
        in_specs=[pl.BlockSpec((rows,1),lambda h:(0,0))]+[pl.BlockSpec((rows,PAIR),lambda h,j=j:(0,h+first+j*pairs)) for j in range(3)]
          +[pl.BlockSpec((rows,PAIR),col),pl.BlockSpec((rows,PAIR),col),pl.BlockSpec((None,rows,2),lambda h:(h+first,0,0))],
        out_specs=[pl.BlockSpec((rows,PAIR),lambda h:(0,h))]*3,
        out_shape=[jax.ShapeDtypeStruct((rows,n*PAIR),BF)]*3,
        scratch_shapes=[pltpu.VMEM((rows,PAIR),BF)]*4+[pltpu.VMEM((rows,PAIR),F32)],
        compiler_params=pltpu.CompilerParams(vmem_limit_bytes=60<<20),
        cost_estimate=pl.CostEstimate(flops=10*rows*rows*PAIR*n*2,bytes_accessed=rows*PAIR*n*16,transcendentals=rows*rows*n*2),
        name="attend_back")(doc,qkv,qkv,qkv,att,datt,lse)

norm_eps = 1e-12


def normalize(values, gain, shift):
    center = values - jnp.mean(values, axis=-1, keepdims=True)
    spread = jnp.mean(center * center, axis=-1, keepdims=True)
    rstd = lax.rsqrt(spread + norm_eps)
    hat = center * rstd
    return hat * gain.astype(F32) + shift.astype(F32), hat, rstd


def normalize_back(grad_out, hat, rstd, gain):
    scaled = grad_out * gain.astype(F32)
    first_mean = jnp.mean(scaled, axis=-1, keepdims=True)
    second_mean = jnp.mean(scaled * hat, axis=-1, keepdims=True)
    return rstd * (scaled - first_mean - hat * second_mean)


def gelu_slope(values):
    cumulative = 0.5 * (1.0 + lax.erf(values * (1.0 / math.sqrt(2.0))))
    density = jnp.exp(-0.5 * values * values) * (1.0 / math.sqrt(2.0 * math.pi))
    return cumulative + values * density


def swap(value, axis, mask):
    size = lax.axis_size(axis)
    return lax.ppermute(value, axis, [(i, i ^ mask) for i in range(size)])


def bits_of(count):
    return [1 << i for i in reversed(range(count.bit_length() - 1))]


def pick(flag, low, high):
    return jnp.where(flag == 0, low, high)


def gather_full(shard, owners):
    core = lax.axis_index("seq") & 1
    index = lax.axis_index("fsdp")
    half = shard.shape[1] // 2
    held = pick(core, shard[:, :half], shard[:, half:])[None]
    for bit in bits_of(owners):
        other = swap(held, "fsdp", bit)
        flag = (index // bit) & 1
        held = pick(flag, jnp.stack([held, other], axis=1), jnp.stack([other, held], axis=1))
        held = held.reshape((-1,) + held.shape[2:])
    other = swap(held, "seq", 1)
    return pick(core, jnp.concatenate([held, other], axis=2), jnp.concatenate([other, held], axis=2))


def reduce_to_owner(lower, upper, owners):
    core = lax.axis_index("seq") & 1
    index = lax.axis_index("fsdp")
    parts = [pick(core, lower, upper), swap(pick(core, upper, lower), "seq", 1)]
    for bit in reversed(bits_of(owners)):
        flag = (index // bit) & 1
        pairs = [part.reshape((-1, 2) + part.shape[1:]) for part in parts]
        sent = sum(pick(flag, pair[:, 1], pair[:, 0]).astype(F32) for pair in pairs).astype(BF)
        parts = [pick(flag, pair[:, 0], pair[:, 1]) for pair in pairs]
        parts.append(swap(sent, "fsdp", bit))
    own = sum(part[0].astype(F32) for part in parts).astype(BF)
    total = own.astype(F32) + swap(own, "seq", 2).astype(F32)
    other = swap(total, "seq", 1)
    return pick(core, total, other), pick(core, other, total)


def body(
    tokens, segment_ids, out_cotangent, query_weight, query_bias, key_weight, value_weight, value_bias,
    output_weight, output_bias, attn_gain, attn_shift, inner_weight, inner_bias, outer_weight, outer_bias,
    final_gain, final_shift,
):
    groups = lax.axis_size("seq")
    owners = lax.axis_size("fsdp")
    micro, seq_count, local_len, width = tokens.shape
    assert micro * seq_count == groups
    rows = groups * local_len
    shard = query_weight.shape[0]
    hidden = inner_weight.shape[1]
    wide = hidden // owners

    def to_sequences(value):
        return lax.all_to_all(value.reshape((groups, local_len) + value.shape[3:]), "seq", 0, 0, tiled=True)

    x_rows = to_sequences(tokens).reshape(rows, width)
    doc = to_sequences(segment_ids).reshape(rows, 1)
    small = jnp.concatenate(
        [query_bias, value_bias, output_bias, attn_gain, attn_shift, outer_bias, final_gain, final_shift, inner_bias]
    )
    small = jnp.pad(small, (0, 3 * width - small.shape[0]))[None]
    small = jnp.concatenate([small, jnp.zeros((15, 3 * width), BF)], axis=0)
    shard_a = jnp.concatenate(
        [jnp.concatenate([query_weight, key_weight, value_weight], axis=1), small], axis=0
    )
    full_a = gather_full(shard_a, owners)
    qkv_mat = full_a[:, :shard].reshape(width, 3 * width)
    vectors = full_a[:, shard, :]
    query_vec, value_vec, output_vec, gain_first, shift_first, outer_vec, gain_final, shift_final = (
        vectors[:, i * shard : (i + 1) * shard].reshape(width) for i in range(8)
    )
    inner_vec = vectors[:, 8 * shard : 8 * shard + wide].reshape(hidden)
    full_b = gather_full(jnp.concatenate([inner_weight, output_weight], axis=1), owners)
    inner_mat = full_b[:, :, :hidden].reshape(width, hidden)
    output_mat = full_b[:, :, hidden:].reshape(width, width)
    outer_mat = gather_full(outer_weight, owners).reshape(hidden, width)

    qkv_vec = jnp.concatenate([query_vec, jnp.zeros_like(query_vec), value_vec]).astype(F32)
    qkv = (jnp.dot(x_rows, qkv_mat, preferred_element_type=F32) + qkv_vec).astype(BF)
    attended, logsums = attend(doc, qkv)
    first = x_rows.astype(F32) + dot_nn(attended, output_mat) + output_vec.astype(F32)
    normed, hat_first, rstd_first = normalize(first, gain_first, shift_first)
    normed_low = normed.astype(BF)
    inner = dot_nn(normed_low, inner_mat) + inner_vec.astype(F32)
    active = jax.nn.gelu(inner, approximate=False).astype(BF)
    second = normed + dot_nn(active, outer_mat) + outer_vec.astype(F32)
    result, hat_second, rstd_second = normalize(second, gain_final, shift_final)

    def to_tokens(value):
        moved = lax.all_to_all(value.reshape(groups, local_len, width), "seq", 0, 0, tiled=True)
        return moved.reshape(micro, seq_count, local_len, width)

    layer_out = to_tokens(result.astype(BF))
    grad_out = to_sequences(out_cotangent).reshape(rows, width).astype(F32)
    dsecond = normalize_back(grad_out, hat_second, rstd_second, gain_final)
    dbranch_two = dsecond.astype(BF)
    douter = dot_tn(active, dbranch_two).astype(BF).reshape(owners, 2, wide // 2, width)
    douter_sum = jnp.concatenate(reduce_to_owner(douter[:, 0], douter[:, 1], owners), axis=0)
    dactive = dot_nt(dbranch_two, outer_mat)
    dinner = (dactive * gelu_slope(inner)).astype(BF)
    dinner_mat = dot_tn(normed_low, dinner).astype(BF).reshape(owners, shard, hidden)
    dinner_sum = jnp.concatenate(
        reduce_to_owner(dinner_mat[:, :, : hidden // 2], dinner_mat[:, :, hidden // 2 :], owners), axis=1
    )
    dnormed = dsecond + dot_nt(dinner, inner_mat)
    dfirst = normalize_back(dnormed, hat_first, rstd_first, gain_first)
    dbranch = dfirst.astype(BF)
    dattended = dot_nt(dbranch, output_mat).astype(BF)
    dquery, dkey, dvalue = attend_back(doc, qkv, attended, dattended, logsums)
    dqkv = jnp.concatenate([dquery, dkey, dvalue], axis=1)
    input_grad = to_tokens((dfirst + dot_nt(dqkv, qkv_mat)).astype(BF)).astype(F32)
    dqkv_mat = dot_tn(x_rows, dqkv).astype(BF).reshape(owners, shard, 3 * width)
    doutput = dot_tn(attended, dbranch).astype(BF).reshape(owners, shard, width)

    def column_sum(value):
        return jnp.sum(value.astype(F32), axis=0)

    smalls = (
        column_sum(dquery), column_sum(dvalue), column_sum(dbranch), jnp.sum(dnormed * hat_first, axis=0),
        jnp.sum(dnormed, axis=0), column_sum(dbranch_two), jnp.sum(grad_out * hat_second, axis=0),
        jnp.sum(grad_out, axis=0),
    )
    packed = jnp.concatenate(
        [value.reshape(owners, shard) for value in smalls] + [column_sum(dinner).reshape(owners, wide)], axis=1
    )
    packed = jnp.pad(packed, ((0, 0), (0, 2 * width - packed.shape[1]))).astype(BF).reshape(owners, 2, 1, width)
    packed = jnp.pad(packed, ((0, 0), (0, 0), (0, 15), (0, 0)))
    lower = jnp.concatenate([dqkv_mat[:, :, :width], dqkv_mat[:, :, width : 2 * width], packed[:, 0]], axis=1)
    upper = jnp.concatenate([dqkv_mat[:, :, 2 * width :], doutput, packed[:, 1]], axis=1)
    lower, upper = reduce_to_owner(lower, upper, owners)
    flat = jnp.concatenate([lower[2 * shard], upper[2 * shard]])
    vecs = [flat[i * shard : (i + 1) * shard] for i in range(8)]
    dinner_vec = flat[8 * shard : 8 * shard + wide]
    return (
        layer_out, input_grad, lower[:shard], vecs[0], lower[shard : 2 * shard], upper[:shard], vecs[1],
        upper[shard : 2 * shard], vecs[2], vecs[3], vecs[4], dinner_sum, dinner_vec, douter_sum, vecs[5], vecs[6],
        vecs[7],
    )


def solution(mesh):
    rows = P(None, "fsdp", "seq", None)
    mat = P("fsdp", None)
    vec = P("fsdp")
    return jax.shard_map(
        body,
        mesh=mesh,
        in_specs=(
            rows, P(None, "fsdp", "seq"), rows, mat, vec, mat, mat, vec, mat, vec, vec, vec, mat, vec, mat, vec, vec, vec,
        ),
        out_specs=(rows, rows, mat, vec, mat, mat, vec, mat, vec, vec, vec, mat, vec, mat, vec, vec, vec),
        check_vma=False,
    )
```

```python
import math

import jax
import jax.numpy as jnp
from jax import lax
from jax.experimental import pallas as pl
from jax.experimental.pallas import tpu as pltpu
from jax.sharding import PartitionSpec as P

F32=jnp.float32; BF=jnp.bfloat16
PAIR=128; HD=64; BIG=1e30

def dot_nn(a,b): return lax.dot_general(a,b,(((1,),(0,)),((),())),preferred_element_type=F32)
def dot_nt(a,b): return lax.dot_general(a,b,(((1,),(1,)),((),())),preferred_element_type=F32)
def dot_tn(a,b): return lax.dot_general(a,b,(((0,),(0,)),((),())),preferred_element_type=F32)

def split3(v):
    hi=v.astype(BF); r=v-hi.astype(F32); mid=r.astype(BF); lo=(r-mid.astype(F32)).astype(BF)
    return hi,mid,lo

def fwd_kernel(doc_ref,q_ref,k_ref,v_ref,o_ref,lse_ref,qa,ka,va):
    rows=q_ref.shape[0]
    lane=lax.broadcasted_iota(jnp.int32,(rows,PAIR),1)
    doc=doc_ref[...]
    for h in range(2):
        base=(1-h)*HD
        mine=(lane>=h*HD)&(lane<(h+1)*HD)
        same=(lane-base)==doc
        qa[...]=jnp.where(mine,q_ref[...]*jnp.asarray(0.125,BF),jnp.where(same,1.0,0.0).astype(BF))
        ka[...]=jnp.where(mine,k_ref[...],jnp.where(same|(lane<base)|(lane>=base+8),0.0,-BIG).astype(BF))
        va[...]=jnp.where(mine,v_ref[...],jnp.ones((),BF))
        bq=256
        for i in range(rows//bq):
            sl=slice(i*bq,(i+1)*bq)
            sc=dot_nt(qa[sl,:],ka[...])
            m=jnp.max(sc,axis=1,keepdims=True)
            p=jnp.exp(sc-m).astype(BF)
            o=dot_nn(p,va[...])
            l=o[:,base:base+1]
            lse_ref[sl,h:h+1]=m+jnp.log(l)
            out=(o/l).astype(BF)
            if h==0: o_ref[sl,:]=out
            else: o_ref[sl,:]=jnp.where(lane[sl,:]>=HD,out,o_ref[sl,:])

def attend(doc,qkv,first,n):
    rows=qkv.shape[0]; pairs=qkv.shape[1]//3//PAIR
    return pl.pallas_call(fwd_kernel,grid=(n,),
        in_specs=[pl.BlockSpec((rows,1),lambda h:(0,0))]+[pl.BlockSpec((rows,PAIR),lambda h,j=j:(0,h+first+j*pairs)) for j in range(3)],
        out_specs=[pl.BlockSpec((rows,PAIR),lambda h:(0,h)),pl.BlockSpec((None,rows,2),lambda h:(h,0,0))],
        out_shape=[jax.ShapeDtypeStruct((rows,n*PAIR),BF),jax.ShapeDtypeStruct((n,rows,2),F32)],
        scratch_shapes=[pltpu.VMEM((rows,PAIR),BF)]*3,
        compiler_params=pltpu.CompilerParams(vmem_limit_bytes=60<<20),
        cost_estimate=pl.CostEstimate(flops=16*rows*rows*PAIR*n,bytes_accessed=rows*PAIR*n*8,transcendentals=rows*rows*n*2),
        name="attend")(doc,qkv,qkv,qkv)

def bwd_kernel(doc_ref,q_ref,k_ref,v_ref,o_ref,do_ref,lse_ref,dq_ref,dk_ref,dv_ref,dqsum_ref,dvsum_ref,qa,ka,va,da,dqs):
    rows=q_ref.shape[0]
    lane=lax.broadcasted_iota(jnp.int32,(rows,PAIR),1)
    doc=doc_ref[...]
    dof=do_ref[...].astype(F32)*o_ref[...].astype(F32)
    for h in range(2):
        base=(1-h)*HD
        mine=(lane>=h*HD)&(lane<(h+1)*HD)
        rel=lane-base
        same=rel==doc
        delta=jnp.sum(jnp.where(mine,dof,0.0),axis=1,keepdims=True)
        lh,lm,ll=split3(-lse_ref[:,h:h+1]); dh,dm,dl=split3(-delta)
        one=jnp.ones((),BF); zero=jnp.zeros((),BF)
        aug_q=jnp.where(same,one,zero)
        aug_q=jnp.where(rel==8,lh,jnp.where(rel==9,lm,jnp.where(rel==10,ll,aug_q)))
        aug_k=jnp.where((rel>=0)&(rel<8)&(~same),jnp.asarray(-BIG,BF),zero)
        aug_k=jnp.where((rel>=8)&(rel<11),one,aug_k)
        aug_d=jnp.where(rel==8,dh,jnp.where(rel==9,dm,jnp.where(rel==10,dl,zero)))
        aug_v=jnp.where((rel>=8)&(rel<11),one,zero)
        qa[...]=jnp.where(mine,q_ref[...]*jnp.asarray(0.125,BF),aug_q)
        ka[...]=jnp.where(mine,k_ref[...],aug_k)
        va[...]=jnp.where(mine,v_ref[...],aug_v)
        da[...]=jnp.where(mine,do_ref[...],aug_d)
        bk=256
        for i in range(rows//bk):
            sl=slice(i*bk,(i+1)*bk)
            st=dot_nt(ka[sl,:],qa[...])
            pt=jnp.exp(st)
            dpt=dot_nt(va[sl,:],da[...])
            dst=(pt*dpt).astype(BF)
            dv=dot_nn(pt.astype(BF),da[...])
            dk=dot_nn(dst,qa[...])
            dq=dot_tn(dst,ka[sl,:])
            if i==0: dqs[...]=dq
            else: dqs[...]+=dq
            msl=mine[sl,:]
            if h==0:
                dv_ref[sl,:]=dv.astype(BF); dk_ref[sl,:]=dk.astype(BF)
            else:
                dv_ref[sl,:]=jnp.where(msl,dv.astype(BF),dv_ref[sl,:]); dk_ref[sl,:]=jnp.where(msl,dk.astype(BF),dk_ref[sl,:])
        dqv=(dqs[...]*0.125).astype(BF)
        if h==0: dq_ref[...]=dqv
        else: dq_ref[...]=jnp.where(mine,dqv,dq_ref[...])
    dqsum_ref[...]=jnp.sum(dq_ref[...].astype(F32),axis=0,keepdims=True)
    dvsum_ref[...]=jnp.sum(dv_ref[...].astype(F32),axis=0,keepdims=True)

def attend_back(doc,qkv,att,datt,lse,first,n):
    rows=qkv.shape[0]; pairs=qkv.shape[1]//3//PAIR
    col=lambda h:(0,h+first)
    return pl.pallas_call(bwd_kernel,grid=(n,),
        in_specs=[pl.BlockSpec((rows,1),lambda h:(0,0))]+[pl.BlockSpec((rows,PAIR),lambda h,j=j:(0,h+first+j*pairs)) for j in range(3)]
          +[pl.BlockSpec((rows,PAIR),lambda h:(0,h)),pl.BlockSpec((rows,PAIR),col),pl.BlockSpec((None,rows,2),lambda h:(h,0,0))],
        out_specs=[pl.BlockSpec((rows,PAIR),lambda h:(0,h))]*3+[pl.BlockSpec((1,PAIR),lambda h:(0,h))]*2,
        out_shape=[jax.ShapeDtypeStruct((rows,n*PAIR),BF)]*3+[jax.ShapeDtypeStruct((1,n*PAIR),F32)]*2,
        scratch_shapes=[pltpu.VMEM((rows,PAIR),BF)]*4+[pltpu.VMEM((rows,PAIR),F32)],
        compiler_params=pltpu.CompilerParams(vmem_limit_bytes=60<<20),
        cost_estimate=pl.CostEstimate(flops=24*rows*rows*PAIR*n,bytes_accessed=rows*PAIR*n*16,transcendentals=rows*rows*n*2),
        name="attend_back")(doc,qkv,qkv,qkv,att,datt,lse)

norm_eps = 1e-12
MAT = pl.BlockSpec(memory_space=pl.ANY)
SCALAR = pl.BlockSpec(memory_space=pltpu.SMEM)
LIMIT = 60 << 20


def swap(value, axis, mask):
    size = lax.axis_size(axis)
    return lax.ppermute(value, axis, [(i, i ^ mask) for i in range(size)])


def after(value, *deps):
    return lax.optimization_barrier((value,) + deps)[0]


def pick(flag, low, high):
    return jnp.where(flag == 0, low, high)


def bits_of(count):
    return [1 << i for i in reversed(range(count.bit_length() - 1))]


def order_of(owners):
    masks = [0]
    for bit in bits_of(owners):
        masks = masks + [m ^ bit for m in masks]
    return masks


def absolute(held, owners):
    index = lax.axis_index("fsdp")
    for bit in bits_of(owners):
        other = swap(held, "fsdp", bit)
        flag = (index // bit) & 1
        held = pick(flag, jnp.stack([held, other], axis=1), jnp.stack([other, held], axis=1))
        held = held.reshape((-1,) + held.shape[2:])
    return held


def load(copies, sems):
    started = [pltpu.make_async_copy(src, dst, sems.at[i]) for i, (src, dst) in enumerate(copies)]
    for copy in started:
        copy.start()
    return started


def piece_copies(plan, refs, at_ref, place):
    owner, part = at_ref[0], at_ref[1]
    copies = []
    for (masks, seq_mask), ref in zip(plan, refs):
        if masks is None:
            copies += place(ref, None, part ^ seq_mask)
        else:
            for i, mask in enumerate(masks):
                copies += place(ref.at[i], owner ^ mask, part ^ seq_mask)
    return copies


def project_kernel(plan, shard, at_ref, x_ref, bias_ref, *rest):
    pieces, (out_ref, mat, sems) = rest[:-3], rest[-3:]
    half = mat.shape[1] // 2

    @pl.when(pl.program_id(0) == 0)
    def _():
        for copy in load(qkv_copies(plan, pieces, at_ref, mat, shard), sems):
            copy.wait()

    out_ref[...] = (dot_nn(x_ref[...], mat[...]) + bias_ref[...]).astype(BF)


def columns(part, size):
    return pl.ds(pl.multiple_of(part * size, 128), size)


def lines(owner, size):
    return pl.ds(pl.multiple_of(owner * size, 16), size)


def qkv_copies(plan, refs, at_ref, mat, shard):
    half = mat.shape[1] // 2

    def place(src, owner, part):
        if owner is None:
            return [(src, mat.at[:, columns(part & 1, half)])]
        return [(src, mat.at[lines(owner, shard), columns(part & 1, half)])]

    return piece_copies(plan, refs, at_ref, place)


def project(at, x_rows, bias, plan, pieces, shard):
    rows, width = x_rows.shape
    blocks = 4
    count = sum(1 if masks is None else len(masks) for masks, _ in plan)
    return pl.pallas_call(
        lambda *refs: project_kernel(plan, shard, *refs),
        grid=(blocks,),
        in_specs=[SCALAR, pl.BlockSpec((rows // blocks, width), lambda i: (i, 0)), pl.BlockSpec((1, 3 * width), lambda i: (0, 0))]
        + [MAT] * len(pieces),
        out_specs=pl.BlockSpec((rows // blocks, 3 * width), lambda i: (i, 0)),
        out_shape=jax.ShapeDtypeStruct((rows, 3 * width), BF),
        scratch_shapes=[pltpu.VMEM((width, 3 * width), BF), pltpu.SemaphoreType.DMA((count,))],
        compiler_params=pltpu.CompilerParams(vmem_limit_bytes=LIMIT),
        cost_estimate=pl.CostEstimate(flops=6 * rows * width * width, bytes_accessed=14 * rows * width, transcendentals=0),
        name="project",
    )(at, x_rows, bias, *pieces)


def mean_of(value):
    return jnp.mean(value, axis=-1, keepdims=True)


def ffn_kernel(plans, shard, at_ref, x_ref, gout_ref, vec_ref, bias_ref, *rest):
    count_att = plans[2]
    atts, rest = rest[:count_att], rest[count_att:]
    inner_pieces, rest = rest[: len(plans[0])], rest[len(plans[0]) :]
    outer_pieces, rest = rest[: len(plans[1])], rest[len(plans[1]) :]
    (
        res_ref, act_ref, din_ref, low_ref, db2_ref, db_ref, dfirst_ref, datt_ref, sums_ref, dsum_ref,
        w1, wo, w2, slope, sem_a, sem_b,
    ) = rest
    width, hidden = w1.shape
    step = pl.program_id(0)

    @pl.when(step == 0)
    def _():
        def place(src, owner, part):
            if owner is None:
                rows = slice(None)
            else:
                rows = lines(owner, shard)
            part = part & 1
            return [
                (src.at[:, : hidden // 2], w1.at[rows, columns(part, hidden // 2)]),
                (src.at[:, hidden // 2 :], wo.at[rows, columns(part, width // 2)]),
            ]

        def place_outer(src, owner, part):
            if owner is None:
                return [(src, w2)]
            size = src.shape[0]
            return [(src, w2.at[lines(owner * 4 + part, size)])]

        first = load(piece_copies(plans[0], inner_pieces, at_ref, place), sem_a)
        later = load(piece_copies(plans[1], outer_pieces, at_ref, place_outer), sem_b)
        for copy in first + later:
            copy.wait()
        sums_ref[...] = jnp.zeros_like(sums_ref)
        dsum_ref[...] = jnp.zeros_like(dsum_ref)

    output_vec, gain_first, shift_first, outer_vec, gain_final, shift_final = (
        vec_ref[i : i + 1, :] for i in range(6)
    )
    wide = atts[0].shape[1]
    first = x_ref[...].astype(F32) + output_vec
    for i, att in enumerate(atts):
        first = first + dot_nn(att[...], wo[i * wide : (i + 1) * wide, :])
    center = first - mean_of(first)
    rstd1 = lax.rsqrt(mean_of(center * center) + norm_eps)
    hat1 = center * rstd1
    normed = hat1 * gain_first + shift_first
    low = normed.astype(BF)
    low_ref[...] = low
    chunk = 768
    second = normed + outer_vec
    for start in range(0, hidden, chunk):
        sl = slice(start, start + chunk)
        inner = dot_nn(low, w1[:, sl]) + bias_ref[:, sl]
        cdf = 0.5 * (1.0 + lax.erf(inner * (1.0 / math.sqrt(2.0))))
        act = (inner * cdf).astype(BF)
        slope[:, sl] = cdf + inner * (jnp.exp(-0.5 * inner * inner) * (1.0 / math.sqrt(2.0 * math.pi)))
        act_ref[:, sl] = act
        second = second + dot_nn(act, w2[sl, :])
    center = second - mean_of(second)
    rstd2 = lax.rsqrt(mean_of(center * center) + norm_eps)
    hat2 = center * rstd2
    res_ref[...] = (hat2 * gain_final + shift_final).astype(BF)
    gout = gout_ref[...].astype(F32)
    scaled = gout * gain_final
    dsecond = rstd2 * (scaled - mean_of(scaled) - hat2 * mean_of(scaled * hat2))
    db2 = dsecond.astype(BF)
    db2_ref[...] = db2
    dnormed = dsecond
    for start in range(0, hidden, chunk):
        sl = slice(start, start + chunk)
        dinner = (dot_nt(db2, w2[sl, :]) * slope[:, sl]).astype(BF)
        din_ref[:, sl] = dinner
        dsum_ref[:, sl] += jnp.sum(dinner.astype(F32), axis=0, keepdims=True)
        dnormed = dnormed + dot_nt(dinner, w1[:, sl])
    scaled = dnormed * gain_first
    dfirst = rstd1 * (scaled - mean_of(scaled) - hat1 * mean_of(scaled * hat1))
    dfirst_ref[...] = dfirst
    db = dfirst.astype(BF)
    db_ref[...] = db
    datt_ref[...] = dot_nt(db, wo[...]).astype(BF)

    def total(value):
        return jnp.sum(value, axis=0, keepdims=True)

    parts = (db.astype(F32), dnormed * hat1, dnormed, db2.astype(F32), gout * hat2, gout)
    for i, value in enumerate(parts):
        sums_ref[i : i + 1, :] += total(value)


def ffn(at, x_rows, gout, vecs, bias, atts, inner_plan, inner_pieces, outer_plan, outer_pieces, shard):
    rows, width = x_rows.shape
    hidden = bias.shape[1]
    blocks = 4
    tall = rows // blocks

    def row(cols):
        return pl.BlockSpec((tall, cols), lambda i: (i, 0))

    def whole(shape):
        return pl.BlockSpec(shape, lambda i: (0, 0))

    def count(plan, times):
        return times * sum(1 if masks is None else len(masks) for masks, _ in plan)

    shape = jax.ShapeDtypeStruct
    return pl.pallas_call(
        lambda *refs: ffn_kernel((inner_plan, outer_plan, len(atts)), shard, *refs),
        grid=(blocks,),
        in_specs=[SCALAR, row(width), row(width), whole(vecs.shape), whole(bias.shape)]
        + [row(att.shape[1]) for att in atts]
        + [MAT] * (len(inner_pieces) + len(outer_pieces)),
        out_specs=[
            row(width), row(hidden), row(hidden), row(width), row(width), row(width), row(width), row(width),
            whole((8, width)), whole((1, hidden)),
        ],
        out_shape=[
            shape((rows, width), BF), shape((rows, hidden), BF), shape((rows, hidden), BF), shape((rows, width), BF),
            shape((rows, width), BF), shape((rows, width), BF), shape((rows, width), F32), shape((rows, width), BF),
            shape((8, width), F32), shape((1, hidden), F32),
        ],
        scratch_shapes=[
            pltpu.VMEM((width, hidden), BF), pltpu.VMEM((width, width), BF), pltpu.VMEM((hidden, width), BF),
            pltpu.VMEM((tall, hidden), F32), pltpu.SemaphoreType.DMA((count(inner_plan, 2),)),
            pltpu.SemaphoreType.DMA((count(outer_plan, 1),)),
        ],
        compiler_params=pltpu.CompilerParams(vmem_limit_bytes=LIMIT),
        cost_estimate=pl.CostEstimate(
            flops=4 * rows * width * (2 * hidden + width), bytes_accessed=rows * (4 * hidden + 20 * width), transcendentals=2 * rows * hidden
        ),
        name="ffn",
    )(at, x_rows, gout, vecs, bias, *atts, *inner_pieces, *outer_pieces)


def grad_kernel(masks, extra_ref, at_ref, *refs):
    left_ref, rights, (keep_ref, send_ref, done) = refs[0], refs[1:-3], refs[-3:]
    step = pl.program_id(0)
    for number, right in enumerate(rights):
        @pl.when(step == number)
        def _(right=right):
            done[...] = dot_tn(left_ref[...], right[...]).astype(BF)

    size = done.shape[0] // len(masks)
    half = size // 2
    owner, core = at_ref[0], at_ref[1] & 1
    for i, mask in enumerate(masks):
        base = (owner ^ mask) * size
        keep_ref[i, :half] = done[pl.ds(pl.multiple_of(base + core * half, 16), half), :]
        send_ref[i, :half] = done[pl.ds(pl.multiple_of(base + (1 - core) * half, 16), half), :]
        if extra_ref is not None:
            more = jnp.where(step == 0, extra_ref[owner ^ mask], jnp.zeros((), BF))
            keep_ref[i, half:] = more
            send_ref[i, half:] = more


def grad_wide(at, masks, left, rights, extra=None):
    rows, width = left.shape
    steps = len(rights)
    chunk = rights[0].shape[1]
    lines_out = width // len(masks) // 2 + (0 if extra is None else extra.shape[1])
    whole = [pl.BlockSpec((rows, width), lambda i: (0, 0))] + [pl.BlockSpec((rows, chunk), lambda i: (0, 0))] * steps
    extras = [] if extra is None else [extra]
    extra_specs = [pl.BlockSpec(value.shape, lambda i: (0, 0, 0)) for value in extras]
    out = jax.ShapeDtypeStruct((len(masks), lines_out, steps * chunk), BF)
    spec = pl.BlockSpec((len(masks), lines_out, chunk), lambda i: (0, 0, i))

    def kernel(at_ref, *refs):
        if extra is None:
            grad_kernel(masks, None, at_ref, *refs)
        else:
            grad_kernel(masks, refs[0], at_ref, *refs[1:])

    return pl.pallas_call(
        kernel,
        grid=(steps,),
        in_specs=[SCALAR] + extra_specs + whole,
        out_specs=[spec, spec],
        out_shape=[out, out],
        scratch_shapes=[pltpu.VMEM((width, chunk), BF)],
        compiler_params=pltpu.CompilerParams(vmem_limit_bytes=LIMIT),
        cost_estimate=pl.CostEstimate(flops=2 * rows * width * steps * chunk, bytes_accessed=2 * steps * chunk * (rows + width), transcendentals=0),
        name="grad_wide",
    )(at, *extras, left, *rights)


def grad_inner_kernel(masks, at_ref, low_ref, din_ref, att_refs, db_ref, outs, done):
    step = pl.program_id(0)
    last = pl.num_programs(0) - 1
    size = done.shape[0] // len(masks)
    half = size // 2
    wide = done.shape[1] // 2

    @pl.when(step < last)
    def _():
        done[...] = dot_tn(low_ref[...], din_ref[...]).astype(BF)

    @pl.when(step == last)
    def _():
        cols = att_refs[0].shape[1]
        for i, att in enumerate(att_refs):
            done[i * cols : (i + 1) * cols, :] = dot_tn(att[...], db_ref[...]).astype(BF)

    owner, core, side = at_ref[0], at_ref[1] & 1, at_ref[1] >> 1
    for i, mask in enumerate(masks):
        base = (owner ^ mask) * size
        for j, (other_core, other_side) in enumerate(((0, 0), (0, 1), (1, 0), (1, 1))):
            line = pl.multiple_of(base + (core ^ other_core) * half, 16)
            column = pl.multiple_of((side ^ other_side) * wide, 128)
            outs[j][i] = done[pl.ds(line, half), pl.ds(column, wide)]


def grad_inner(at, masks, low, dinner, atts, db):
    rows, width = low.shape
    hidden = dinner.shape[1]
    chunk = width
    steps = hidden // chunk + 1
    size = width // len(masks)
    whole = pl.BlockSpec((rows, width), lambda i: (0, 0))
    out = jax.ShapeDtypeStruct((len(masks), size // 2, steps * chunk // 2), BF)
    spec = pl.BlockSpec((len(masks), size // 2, chunk // 2), lambda i: (0, 0, i))
    n = len(atts)
    return pl.pallas_call(
        lambda at_ref, low_ref, din_ref, *refs: grad_inner_kernel(
            masks, at_ref, low_ref, din_ref, refs[:n], refs[n], refs[n + 1 : n + 5], refs[n + 5]
        ),
        grid=(steps,),
        in_specs=[SCALAR, whole, pl.BlockSpec((rows, chunk), lambda i: (0, jnp.minimum(i, steps - 2)))]
        + [pl.BlockSpec((rows, att.shape[1]), lambda i: (0, 0)) for att in atts]
        + [whole],
        out_specs=[spec] * 4,
        out_shape=[out] * 4,
        scratch_shapes=[pltpu.VMEM((width, chunk), BF)],
        compiler_params=pltpu.CompilerParams(vmem_limit_bytes=LIMIT),
        cost_estimate=pl.CostEstimate(flops=2 * rows * width * (hidden + width), bytes_accessed=4 * rows * hidden, transcendentals=0),
        name="grad_inner",
    )(at, low, dinner, *atts, db)


def grad_outer_kernel(half, at_ref, act_ref, db2_ref, keep_ref, send_ref, done):
    core = at_ref[1] & 1
    done[...] = dot_tn(act_ref[...], db2_ref[...]).astype(BF)
    keep_ref[0] = done[pl.ds(pl.multiple_of(core * half, 16), half), :]
    send_ref[0] = done[pl.ds(pl.multiple_of((1 - core) * half, 16), half), :]


def grad_outer(at, owners, act, db2):
    rows, hidden = act.shape
    width = db2.shape[1]
    size = hidden // owners
    levels = owners.bit_length() - 1

    def column(i, at_ref):
        mask = 0
        for level in range(levels):
            mask = mask | (((i >> level) & 1) << (levels - 1 - level))
        return (0, at_ref[0] ^ mask)

    out = jax.ShapeDtypeStruct((owners, size // 2, width), BF)
    spec = pl.BlockSpec((1, size // 2, width), lambda i, at_ref: (i, 0, 0))
    return pl.pallas_call(
        lambda *refs: grad_outer_kernel(size // 2, *refs),
        grid_spec=pltpu.PrefetchScalarGridSpec(
            num_scalar_prefetch=1,
            grid=(owners,),
            in_specs=[pl.BlockSpec((rows, size), column), pl.BlockSpec((rows, width), lambda i, at_ref: (0, 0))],
            out_specs=[spec, spec],
            scratch_shapes=[pltpu.VMEM((size, width), BF)],
        ),
        out_shape=[out, out],
        compiler_params=pltpu.CompilerParams(vmem_limit_bytes=LIMIT),
        cost_estimate=pl.CostEstimate(flops=2 * rows * width * hidden, bytes_accessed=4 * rows * hidden, transcendentals=0),
        name="grad_outer",
    )(at, act, db2)


def input_kernel(plan, shard, count, at_ref, dfirst_ref, *rest):
    parts, rest = rest[:count], rest[count:]
    pieces, (out_ref, mat, sems) = rest[:-3], rest[-3:]

    @pl.when(pl.program_id(0) == 0)
    def _():
        for copy in load(qkv_copies(plan, pieces, at_ref, mat, shard), sems):
            copy.wait()

    width = mat.shape[0]
    wide = parts[0].shape[1]
    total = dfirst_ref[...]
    for i, part in enumerate(parts):
        start = (i % 3) * width + (i // 3) * wide
        total = total + dot_nt(part[...], mat[:, start : start + wide])
    out_ref[...] = total.astype(BF)


def input_gradient(at, dfirst, parts, plan, pieces, shard):
    rows, width = dfirst.shape
    blocks = 4
    count = sum(1 if masks is None else len(masks) for masks, _ in plan)

    def row(cols):
        return pl.BlockSpec((rows // blocks, cols), lambda i: (i, 0))

    return pl.pallas_call(
        lambda *refs: input_kernel(plan, shard, len(parts), *refs),
        grid=(blocks,),
        in_specs=[SCALAR, row(width)] + [row(part.shape[1]) for part in parts] + [MAT] * len(pieces),
        out_specs=row(width),
        out_shape=jax.ShapeDtypeStruct((rows, width), BF),
        scratch_shapes=[pltpu.VMEM((width, 3 * width), BF), pltpu.SemaphoreType.DMA((count,))],
        compiler_params=pltpu.CompilerParams(vmem_limit_bytes=LIMIT),
        cost_estimate=pl.CostEstimate(flops=6 * rows * width * width, bytes_accessed=14 * rows * width, transcendentals=0),
        name="input_gradient",
    )(at, dfirst, *parts, *pieces)


def column_sum(value):
    return jnp.sum(value.astype(F32), axis=0)


def fold(parts):
    return sum(part.astype(F32) for part in parts)


def halve(parts):
    half = parts[0].shape[0] // 2
    return fold([part[half:] for part in parts]).astype(BF), [part[:half] for part in parts]


def reduce_to_owner(value, owners):
    index = lax.axis_index("fsdp")
    parts = [value]
    for bit in reversed(bits_of(owners)):
        flag = (index // bit) & 1
        pairs = [part.reshape((-1, 2) + part.shape[1:]) for part in parts]
        sent = fold([pick(flag, pair[:, 1], pair[:, 0]) for pair in pairs]).astype(BF)
        parts = [pick(flag, pair[:, 0], pair[:, 1]) for pair in pairs] + [swap(sent, "fsdp", bit)]
    total = fold([part[0] for part in parts])
    for bit in (1, 2):
        own = total.astype(BF)
        total = own.astype(F32) + swap(own, "seq", bit).astype(F32)
    return total


def body(
    tokens, segment_ids, out_cotangent, query_weight, query_bias, key_weight, value_weight, value_bias,
    output_weight, output_bias, attn_gain, attn_shift, inner_weight, inner_bias, outer_weight, outer_bias,
    final_gain, final_shift,
):
    groups = lax.axis_size("seq")
    owners = lax.axis_size("fsdp")
    micro, seq_count, local_len, width = tokens.shape
    assert micro * seq_count == groups == 4
    rows = groups * local_len
    shard = query_weight.shape[0]
    hidden = inner_weight.shape[1]
    wide = hidden // owners
    lots = wide // shard
    aligned = shard % 32 == 0 and owners == 8
    place = lax.axis_index("seq")
    core = place & 1
    at = jnp.stack([lax.axis_index("fsdp"), place]).astype(jnp.int32)
    masks = order_of(owners)

    def to_sequences(value):
        return lax.all_to_all(value.reshape((groups, local_len) + value.shape[3:]), "seq", 0, 0, tiled=True)

    def to_tokens(value):
        moved = lax.all_to_all(value.reshape(groups, local_len, width), "seq", 0, 0, tiled=True)
        return moved.reshape(micro, seq_count, local_len, width)

    small = jnp.stack(
        [query_bias, value_bias, output_bias, attn_gain, attn_shift, outer_bias, final_gain, final_shift]
        + [inner_bias[i * shard : (i + 1) * shard] for i in range(lots)]
    )
    piece_a = pick(
        core,
        jnp.concatenate([query_weight, key_weight[:, : width // 2]], axis=1),
        jnp.concatenate([key_weight[:, width // 2 :], value_weight], axis=1),
    )
    piece_b = pick(
        core,
        jnp.concatenate([inner_weight[:, : hidden // 2], output_weight[:, : width // 2]], axis=1),
        jnp.concatenate([inner_weight[:, hidden // 2 :], output_weight[:, width // 2 :]], axis=1),
    )
    if aligned:
        a_far = swap(piece_a[None], "fsdp", 4)
        small_full = absolute(small[None], owners)
        x_rows = to_sequences(tokens).reshape(rows, width)
        doc = to_sequences(segment_ids).reshape(rows, 1)
        a_low = jnp.concatenate([piece_a[None], a_far])
        a_two = swap(a_low, "fsdp", 2)
        a_one = swap(a_low, "fsdp", 1)
        quarter = wide // 4
        piece_c = lax.dynamic_slice(outer_weight, (place * quarter, 0), (quarter, width))[None]
        c_far = swap(after(piece_c, a_two), "fsdp", 4)
        a_three = swap(a_two, "fsdp", 1)
        a_mine = [a_low, a_two, a_one, a_three]
        a_other = [swap(value, "seq", 1) for value in a_mine]
        quads = [(0, 4), (2, 6), (1, 5), (3, 7)]
        plan_a = [(quad, 0) for quad in quads] + [(quad, 1) for quad in quads]
        pieces_a = a_mine + a_other
    else:
        small_full = absolute(small[None], owners)
        x_rows = to_sequences(tokens).reshape(rows, width)
        doc = to_sequences(segment_ids).reshape(rows, 1)
        mine = absolute(piece_a[None], owners).reshape(width, -1)
        plan_a = [(None, 0), (None, 1)]
        pieces_a = [mine, swap(mine, "seq", 1)]
    small_full = small_full.astype(F32)
    vecs = small_full[:, :8].transpose(1, 0, 2).reshape(8, width)
    inner_vec = small_full[:, 8:].reshape(1, hidden)
    qkv_vec = jnp.concatenate([vecs[0:1], jnp.zeros((1, width), F32), vecs[1:2]], axis=1)
    ffn_vecs = vecs[2:]

    if aligned:
        qkv = project(at, after(x_rows, c_far), qkv_vec, plan_a, pieces_a, shard)
    else:
        qkv = project(at, x_rows, qkv_vec, plan_a, pieces_a, shard)
    pairs = width // PAIR
    calls = 3
    each = pairs // calls
    atts, logs = [], []
    if aligned:
        c_low = jnp.concatenate([piece_c, c_far])
        c_two = swap(c_low, "fsdp", 2)
        c_one = swap(c_low, "fsdp", 1)
        b_far = swap(after(piece_b, c_far)[None], "fsdp", 4)
        qkv = after(qkv, c_two, c_one)
        att, log = attend(doc, qkv, 0, each)
        atts.append(att)
        logs.append(log)
        c_three = swap(c_two, "fsdp", 1)
        c_side = [swap(c_low, "seq", 2), swap(c_two, "seq", 2)]
        b_low = jnp.concatenate([piece_b[None], b_far])
        qkv, _ = lax.optimization_barrier((qkv, (att, b_low, c_three, c_side)))
        att, log = attend(doc, qkv, each, each)
        atts.append(att)
        logs.append(log)
        b_two = swap(b_low, "fsdp", 2)
        b_one = swap(b_low, "fsdp", 1)
        c_side += [swap(c_one, "seq", 2), swap(c_three, "seq", 2)]
        grads_in = to_sequences(out_cotangent).reshape(rows, width)
        qkv, _ = lax.optimization_barrier((qkv, (att, b_two, b_one, c_side)))
        att, log = attend(doc, qkv, 2 * each, each)
        atts.append(att)
        logs.append(log)
        b_three = swap(b_two, "fsdp", 1)
        b_mine = [b_low, b_two, b_one, b_three]
        b_other = [swap(value, "seq", 1) for value in b_mine]
        plan_b, pieces_b = plan_a, b_mine + b_other
        c_mine = [c_low, c_two, c_one, c_three]
        c_all = c_mine + c_side
        plan_c = [(quad, mask) for mask in (0, 2, 1, 3) for quad in quads]
        pieces_c = c_all + [swap(value, "seq", 1) for value in c_all]
    else:
        for call in range(calls):
            att, log = attend(doc, qkv, call * each, each)
            atts.append(att)
            logs.append(log)
        grads_in = to_sequences(out_cotangent).reshape(rows, width)
        mine = absolute(piece_b[None], owners).reshape(width, -1)
        plan_b, pieces_b = plan_a, [mine, swap(mine, "seq", 1)]
        plan_c, pieces_c = [(None, 0)], [absolute(outer_weight[None], owners).reshape(hidden, width)]
    result, active, dinner, low, db2, db, dfirst, dattended, sums, dinner_vec = ffn(
        at, x_rows, grads_in, ffn_vecs, inner_vec, atts, plan_b, pieces_b, plan_c, pieces_c, shard
    )
    layer_out = to_tokens(result)

    backs = []

    def back(call, gate):
        return attend_back(doc, qkv, atts[call], gate, logs[call], call * each, each)

    def vectors():
        dq = jnp.concatenate([one[3] for one in backs], axis=1)
        dv = jnp.concatenate([one[4] for one in backs], axis=1)
        eight = jnp.concatenate([dq, dv, sums[:6]]).reshape(8, owners, shard).transpose(1, 0, 2)
        return jnp.concatenate([eight, dinner_vec.reshape(owners, lots, shard)], axis=1)

    if aligned:
        outer_keep, outer_send = grad_outer(at, owners, active, db2)
        outer_parts = [outer_keep, swap(outer_send, "seq", 1)]
        inner_kept, inner_side, inner_core, inner_both = grad_inner(at, masks, after(low, outer_keep), dinner, atts, db)
        outer_x, outer_parts = halve(outer_parts)
        gate = after(dattended, inner_kept, outer_x)
        backs.append(back(0, gate))
        outer_parts.append(swap(outer_x, "fsdp", 1))
        inner_parts = [inner_kept, swap(inner_core, "seq", 1)]
        inner_y = fold([inner_side, swap(inner_both, "seq", 1)]).astype(BF)
        gate, _ = lax.optimization_barrier((gate, (backs[0], inner_y, inner_parts)))
        backs.append(back(1, gate))
        inner_parts.append(swap(inner_y, "seq", 2))
        both = [jnp.concatenate([one[j] for one in backs], axis=1) for j in range(3)]
        first_keep, first_send = grad_wide(at, masks, x_rows, both)
        outer_z, outer_parts = halve(outer_parts)
        gate, _ = lax.optimization_barrier((gate, (first_keep, outer_z)))
        backs.append(back(2, gate))
        outer_parts.append(swap(outer_z, "fsdp", 2))
        first_parts = [first_keep, swap(first_send, "seq", 1)]
        outer_zz, outer_parts = halve(outer_parts)
        inner_x, inner_parts = halve(inner_parts)
        first_x, first_parts = halve(first_parts)
        extra = vectors()
        extra = jnp.pad(extra, ((0, 0), (0, 16 - extra.shape[1]), (0, each * PAIR - shard))).astype(BF)
        gated, _ = lax.optimization_barrier((x_rows, (outer_zz, inner_x, first_x)))
        second_keep, second_send = grad_wide(at, masks, gated, backs[2][:3], extra)
        dfirst, _ = lax.optimization_barrier((dfirst, (second_keep,)))
        parts = [value for one in backs for value in one[:3]]
        moved = input_gradient(at, dfirst, parts, plan_a, pieces_a, shard)
        input_grad = to_tokens(moved).astype(F32)
        outer_parts.append(swap(outer_zz, "fsdp", 4))
        inner_parts.append(swap(inner_x, "fsdp", 1))
        first_parts.append(swap(first_x, "fsdp", 1))
        second_parts = [second_keep, swap(second_send, "seq", 1)]
        second_x, second_parts = halve(second_parts)
        second_parts.append(swap(second_x, "fsdp", 1))
        groups_left = [inner_parts, first_parts, second_parts]
        for bit in (2, 4):
            sends = [halve(group) for group in groups_left]
            groups_left = [keep + [swap(sent, "fsdp", bit)] for sent, keep in sends]
        owns = [fold([part[0] for part in group]).astype(BF) for group in [outer_parts] + groups_left]
        others = [swap(own, "seq", 2) for own in owns]
        outer_own, first_own, second_own = (
            owns[i].astype(F32) + others[i].astype(F32) for i in (0, 2, 3)
        )
        side = place >> 1
        half = shard // 2
        cols = width // 2
        inner_own = pick(
            side,
            jnp.stack([value.reshape(half, -1, cols) for value in (owns[1], others[1])], axis=2),
            jnp.stack([value.reshape(half, -1, cols) for value in (others[1], owns[1])], axis=2),
        ).reshape(half, hidden + width)

        def whole(own):
            other = swap(own, "seq", 1)
            return pick(core, jnp.concatenate([own, other]), jnp.concatenate([other, own])).astype(F32)

        douter = whole(outer_own)
        dinner_full = whole(inner_own)
        part = 2 * each * PAIR
        firsts = whole(first_own)
        seconds = whole(second_own[:half])
        rest = each * PAIR
        dqkv = [
            jnp.concatenate([firsts[:, i * part : (i + 1) * part], seconds[:, i * rest : (i + 1) * rest]], axis=1)
            for i in range(3)
        ]
        vec = second_own[half : half + 8 + lots, :shard]
        dinner_w, doutput = dinner_full[:, :hidden], dinner_full[:, hidden:]
    else:
        for call in range(calls):
            backs.append(back(call, dattended))
        parts = [value for one in backs for value in one[:3]]
        moved = input_gradient(at, dfirst, parts, plan_a, pieces_a, shard)
        input_grad = to_tokens(moved).astype(F32)
        three = [jnp.concatenate([one[j] for one in backs], axis=1) for j in range(3)]
        att = jnp.concatenate(atts, axis=1)
        lefts = [x_rows, x_rows, x_rows, att, low]
        rights = three + [db, dinner]
        dqkv = []
        for left, right in zip(lefts, rights):
            dqkv.append(reduce_to_owner(dot_tn(left, right).astype(BF).reshape(owners, shard, -1), owners))
        doutput, dinner_w = dqkv[3:]
        douter = reduce_to_owner(dot_tn(active, db2).astype(BF).reshape(owners, wide, width), owners)
        vec = reduce_to_owner(vectors().astype(BF), owners)
    return (
        layer_out, input_grad, dqkv[0], vec[0], dqkv[1], dqkv[2], vec[1], doutput, vec[2], vec[3], vec[4], dinner_w,
        vec[8:].reshape(wide), douter, vec[5], vec[6], vec[7],
    )


def solution(mesh):
    rows = P(None, "fsdp", "seq", None)
    mat = P("fsdp", None)
    vec = P("fsdp")
    return jax.shard_map(
        body,
        mesh=mesh,
        in_specs=(
            rows, P(None, "fsdp", "seq"), rows, mat, vec, mat, mat, vec, mat, vec, vec, vec, mat, vec, mat, vec, vec, vec,
        ),
        out_specs=(rows, rows, mat, vec, mat, mat, vec, mat, vec, vec, vec, mat, vec, mat, vec, vec, vec),
        check_vma=False,
    )
```

```python
import math

import jax
import jax.numpy as jnp
from jax import lax
from jax.experimental import pallas as pl
from jax.experimental.pallas import tpu as pltpu
from jax.sharding import PartitionSpec as P

F32=jnp.float32; BF=jnp.bfloat16
PAIR=128; HD=64; BIG=1e30

def dot_nn(a,b): return lax.dot_general(a,b,(((1,),(0,)),((),())),preferred_element_type=F32)
def dot_nt(a,b): return lax.dot_general(a,b,(((1,),(1,)),((),())),preferred_element_type=F32)
def dot_tn(a,b): return lax.dot_general(a,b,(((0,),(0,)),((),())),preferred_element_type=F32)

def split3(v):
    hi=v.astype(BF); r=v-hi.astype(F32); mid=r.astype(BF); lo=(r-mid.astype(F32)).astype(BF)
    return hi,mid,lo

def fwd_kernel(doc_ref,q_ref,k_ref,v_ref,o_ref,lse_ref,qa,ka,va):
    rows=q_ref.shape[0]
    lane=lax.broadcasted_iota(jnp.int32,(rows,PAIR),1)
    doc=doc_ref[...]
    for h in range(2):
        base=(1-h)*HD
        mine=(lane>=h*HD)&(lane<(h+1)*HD)
        same=(lane-base)==doc
        qa[...]=jnp.where(mine,q_ref[...]*jnp.asarray(0.125,BF),jnp.where(same,1.0,0.0).astype(BF))
        ka[...]=jnp.where(mine,k_ref[...],jnp.where(same|(lane<base)|(lane>=base+8),0.0,-BIG).astype(BF))
        va[...]=jnp.where(mine,v_ref[...],jnp.ones((),BF))
        bq=256
        for i in range(rows//bq):
            sl=slice(i*bq,(i+1)*bq)
            sc=dot_nt(qa[sl,:],ka[...])
            m=jnp.max(sc,axis=1,keepdims=True)
            p=jnp.exp(sc-m).astype(BF)
            o=dot_nn(p,va[...])
            l=o[:,base:base+1]
            lse_ref[sl,h:h+1]=m+jnp.log(l)
            out=(o/l).astype(BF)
            if h==0: o_ref[sl,:]=out
            else: o_ref[sl,:]=jnp.where(lane[sl,:]>=HD,out,o_ref[sl,:])

def attend(doc,qkv,first,n):
    rows=qkv.shape[0]; pairs=qkv.shape[1]//3//PAIR
    return pl.pallas_call(fwd_kernel,grid=(n,),
        in_specs=[pl.BlockSpec((rows,1),lambda h:(0,0))]+[pl.BlockSpec((rows,PAIR),lambda h,j=j:(0,h+first+j*pairs)) for j in range(3)],
        out_specs=[pl.BlockSpec((rows,PAIR),lambda h:(0,h)),pl.BlockSpec((None,rows,2),lambda h:(h,0,0))],
        out_shape=[jax.ShapeDtypeStruct((rows,n*PAIR),BF),jax.ShapeDtypeStruct((n,rows,2),F32)],
        scratch_shapes=[pltpu.VMEM((rows,PAIR),BF)]*3,
        compiler_params=pltpu.CompilerParams(vmem_limit_bytes=60<<20),
        cost_estimate=pl.CostEstimate(flops=16*rows*rows*PAIR*n,bytes_accessed=rows*PAIR*n*8,transcendentals=rows*rows*n*2),
        name="attend")(doc,qkv,qkv,qkv)

def bwd_kernel(doc_ref,q_ref,k_ref,v_ref,o_ref,do_ref,lse_ref,dq_ref,dk_ref,dv_ref,dqsum_ref,dvsum_ref,qa,ka,va,da,dqs):
    rows=q_ref.shape[0]
    lane=lax.broadcasted_iota(jnp.int32,(rows,PAIR),1)
    doc=doc_ref[...]
    dof=do_ref[...].astype(F32)*o_ref[...].astype(F32)
    for h in range(2):
        base=(1-h)*HD
        mine=(lane>=h*HD)&(lane<(h+1)*HD)
        rel=lane-base
        same=rel==doc
        delta=jnp.sum(jnp.where(mine,dof,0.0),axis=1,keepdims=True)
        lh,lm,ll=split3(-lse_ref[:,h:h+1]); dh,dm,dl=split3(-delta)
        one=jnp.ones((),BF); zero=jnp.zeros((),BF)
        aug_q=jnp.where(same,one,zero)
        aug_q=jnp.where(rel==8,lh,jnp.where(rel==9,lm,jnp.where(rel==10,ll,aug_q)))
        aug_k=jnp.where((rel>=0)&(rel<8)&(~same),jnp.asarray(-BIG,BF),zero)
        aug_k=jnp.where((rel>=8)&(rel<11),one,aug_k)
        aug_d=jnp.where(rel==8,dh,jnp.where(rel==9,dm,jnp.where(rel==10,dl,zero)))
        aug_v=jnp.where((rel>=8)&(rel<11),one,zero)
        qa[...]=jnp.where(mine,q_ref[...]*jnp.asarray(0.125,BF),aug_q)
        ka[...]=jnp.where(mine,k_ref[...],aug_k)
        va[...]=jnp.where(mine,v_ref[...],aug_v)
        da[...]=jnp.where(mine,do_ref[...],aug_d)
        bk=256
        for i in range(rows//bk):
            sl=slice(i*bk,(i+1)*bk)
            st=dot_nt(ka[sl,:],qa[...])
            pt=jnp.exp(st)
            dpt=dot_nt(va[sl,:],da[...])
            dst=(pt*dpt).astype(BF)
            dv=dot_nn(pt.astype(BF),da[...])
            dk=dot_nn(dst,qa[...])
            dq=dot_tn(dst,ka[sl,:])
            if i==0: dqs[...]=dq
            else: dqs[...]+=dq
            msl=mine[sl,:]
            if h==0:
                dv_ref[sl,:]=dv.astype(BF); dk_ref[sl,:]=dk.astype(BF)
            else:
                dv_ref[sl,:]=jnp.where(msl,dv.astype(BF),dv_ref[sl,:]); dk_ref[sl,:]=jnp.where(msl,dk.astype(BF),dk_ref[sl,:])
        dqv=(dqs[...]*0.125).astype(BF)
        if h==0: dq_ref[...]=dqv
        else: dq_ref[...]=jnp.where(mine,dqv,dq_ref[...])
    dqsum_ref[...]=jnp.sum(dq_ref[...].astype(F32),axis=0,keepdims=True)
    dvsum_ref[...]=jnp.sum(dv_ref[...].astype(F32),axis=0,keepdims=True)

def attend_back(doc,qkv,att,datt,lse,first,n):
    rows=qkv.shape[0]; pairs=qkv.shape[1]//3//PAIR
    col=lambda h:(0,h+first)
    return pl.pallas_call(bwd_kernel,grid=(n,),
        in_specs=[pl.BlockSpec((rows,1),lambda h:(0,0))]+[pl.BlockSpec((rows,PAIR),lambda h,j=j:(0,h+first+j*pairs)) for j in range(3)]
          +[pl.BlockSpec((rows,PAIR),lambda h:(0,h)),pl.BlockSpec((rows,PAIR),col),pl.BlockSpec((None,rows,2),lambda h:(h,0,0))],
        out_specs=[pl.BlockSpec((rows,PAIR),lambda h:(0,h))]*3+[pl.BlockSpec((1,PAIR),lambda h:(0,h))]*2,
        out_shape=[jax.ShapeDtypeStruct((rows,n*PAIR),BF)]*3+[jax.ShapeDtypeStruct((1,n*PAIR),F32)]*2,
        scratch_shapes=[pltpu.VMEM((rows,PAIR),BF)]*4+[pltpu.VMEM((rows,PAIR),F32)],
        compiler_params=pltpu.CompilerParams(vmem_limit_bytes=60<<20),
        cost_estimate=pl.CostEstimate(flops=24*rows*rows*PAIR*n,bytes_accessed=rows*PAIR*n*16,transcendentals=rows*rows*n*2),
        name="attend_back")(doc,qkv,qkv,qkv,att,datt,lse)

norm_eps = 1e-12
MAT = pl.BlockSpec(memory_space=pl.ANY)
SCALAR = pl.BlockSpec(memory_space=pltpu.SMEM)
LIMIT = 60 << 20


def swap(value, axis, mask):
    size = lax.axis_size(axis)
    return lax.ppermute(value, axis, [(i, i ^ mask) for i in range(size)])


def after(value, *deps):
    return lax.optimization_barrier((value,) + deps)[0]


def pick(flag, low, high):
    return jnp.where(flag == 0, low, high)


def bits_of(count):
    return [1 << i for i in reversed(range(count.bit_length() - 1))]


def order_of(owners):
    masks = [0]
    for bit in bits_of(owners):
        masks = masks + [m ^ bit for m in masks]
    return masks


def absolute(held, owners):
    index = lax.axis_index("fsdp")
    for bit in bits_of(owners):
        other = swap(held, "fsdp", bit)
        flag = (index // bit) & 1
        held = pick(flag, jnp.stack([held, other], axis=1), jnp.stack([other, held], axis=1))
        held = held.reshape((-1,) + held.shape[2:])
    return held


def load(copies, sems):
    started = [pltpu.make_async_copy(src, dst, sems.at[i]) for i, (src, dst) in enumerate(copies)]
    for copy in started:
        copy.start()
    return started


def piece_copies(plan, refs, at_ref, place):
    owner, part = at_ref[0], at_ref[1]
    copies = []
    for (masks, seq_mask), ref in zip(plan, refs):
        if masks is None:
            copies += place(ref, None, part ^ seq_mask)
        else:
            for i, mask in enumerate(masks):
                copies += place(ref.at[i], owner ^ mask, part ^ seq_mask)
    return copies


def project_kernel(plan, shard, at_ref, x_ref, bias_ref, *rest):
    pieces, (out_ref, mat, sems) = rest[:-3], rest[-3:]
    half = mat.shape[1] // 2

    @pl.when(pl.program_id(0) == 0)
    def _():
        for copy in load(qkv_copies(plan, pieces, at_ref, mat, shard), sems):
            copy.wait()

    out_ref[...] = (dot_nn(x_ref[...], mat[...]) + bias_ref[...]).astype(BF)


def columns(part, size):
    return pl.ds(pl.multiple_of(part * size, 128), size)


def lines(owner, size):
    return pl.ds(pl.multiple_of(owner * size, 16), size)


def qkv_copies(plan, refs, at_ref, mat, shard):
    half = mat.shape[1] // 2

    def place(src, owner, part):
        if owner is None:
            return [(src, mat.at[:, columns(part & 1, half)])]
        return [(src, mat.at[lines(owner, shard), columns(part & 1, half)])]

    return piece_copies(plan, refs, at_ref, place)


def project(at, x_rows, bias, plan, pieces, shard):
    rows, width = x_rows.shape
    blocks = 4
    count = sum(1 if masks is None else len(masks) for masks, _ in plan)
    return pl.pallas_call(
        lambda *refs: project_kernel(plan, shard, *refs),
        grid=(blocks,),
        in_specs=[SCALAR, pl.BlockSpec((rows // blocks, width), lambda i: (i, 0)), pl.BlockSpec((1, 3 * width), lambda i: (0, 0))]
        + [MAT] * len(pieces),
        out_specs=pl.BlockSpec((rows // blocks, 3 * width), lambda i: (i, 0)),
        out_shape=jax.ShapeDtypeStruct((rows, 3 * width), BF),
        scratch_shapes=[pltpu.VMEM((width, 3 * width), BF), pltpu.SemaphoreType.DMA((count,))],
        compiler_params=pltpu.CompilerParams(vmem_limit_bytes=LIMIT),
        cost_estimate=pl.CostEstimate(flops=6 * rows * width * width, bytes_accessed=14 * rows * width, transcendentals=0),
        name="project",
    )(at, x_rows, bias, *pieces)


def mean_of(value):
    return jnp.mean(value, axis=-1, keepdims=True)


def ffn_kernel(plans, shard, at_ref, x_ref, gout_ref, vec_ref, bias_ref, *rest):
    count_att = plans[2]
    atts, rest = rest[:count_att], rest[count_att:]
    inner_pieces, rest = rest[: len(plans[0])], rest[len(plans[0]) :]
    outer_pieces, rest = rest[: len(plans[1])], rest[len(plans[1]) :]
    (
        res_ref, act_ref, din_ref, low_ref, db2_ref, db_ref, dfirst_ref, datt_ref, sums_ref, dsum_ref,
        w1, wo, w2, slope, sem_a, sem_b,
    ) = rest
    width, hidden = w1.shape
    step = pl.program_id(0)

    @pl.when(step == 0)
    def _():
        def place(src, owner, part):
            if owner is None:
                rows = slice(None)
            else:
                rows = lines(owner, shard)
            part = part & 1
            return [
                (src.at[:, : hidden // 2], w1.at[rows, columns(part, hidden // 2)]),
                (src.at[:, hidden // 2 :], wo.at[rows, columns(part, width // 2)]),
            ]

        def place_outer(src, owner, part):
            if owner is None:
                return [(src, w2)]
            size = src.shape[0]
            return [(src, w2.at[lines(owner * 4 + part, size)])]

        first = load(piece_copies(plans[0], inner_pieces, at_ref, place), sem_a)
        later = load(piece_copies(plans[1], outer_pieces, at_ref, place_outer), sem_b)
        for copy in first + later:
            copy.wait()
        sums_ref[...] = jnp.zeros_like(sums_ref)
        dsum_ref[...] = jnp.zeros_like(dsum_ref)

    output_vec, gain_first, shift_first, outer_vec, gain_final, shift_final = (
        vec_ref[i : i + 1, :] for i in range(6)
    )
    wide = atts[0].shape[1]
    first = x_ref[...].astype(F32) + output_vec
    for i, att in enumerate(atts):
        first = first + dot_nn(att[...], wo[i * wide : (i + 1) * wide, :])
    center = first - mean_of(first)
    rstd1 = lax.rsqrt(mean_of(center * center) + norm_eps)
    hat1 = center * rstd1
    normed = hat1 * gain_first + shift_first
    low = normed.astype(BF)
    low_ref[...] = low
    chunk = 768
    second = normed + outer_vec
    for start in range(0, hidden, chunk):
        sl = slice(start, start + chunk)
        inner = dot_nn(low, w1[:, sl]) + bias_ref[:, sl]
        cdf = 0.5 * (1.0 + lax.erf(inner * (1.0 / math.sqrt(2.0))))
        act = (inner * cdf).astype(BF)
        slope[:, sl] = cdf + inner * (jnp.exp(-0.5 * inner * inner) * (1.0 / math.sqrt(2.0 * math.pi)))
        act_ref[:, sl] = act
        second = second + dot_nn(act, w2[sl, :])
    center = second - mean_of(second)
    rstd2 = lax.rsqrt(mean_of(center * center) + norm_eps)
    hat2 = center * rstd2
    res_ref[...] = (hat2 * gain_final + shift_final).astype(BF)
    gout = gout_ref[...].astype(F32)
    scaled = gout * gain_final
    dsecond = rstd2 * (scaled - mean_of(scaled) - hat2 * mean_of(scaled * hat2))
    db2 = dsecond.astype(BF)
    db2_ref[...] = db2
    dnormed = dsecond
    for start in range(0, hidden, chunk):
        sl = slice(start, start + chunk)
        dinner = (dot_nt(db2, w2[sl, :]) * slope[:, sl]).astype(BF)
        din_ref[:, sl] = dinner
        dsum_ref[:, sl] += jnp.sum(dinner.astype(F32), axis=0, keepdims=True)
        dnormed = dnormed + dot_nt(dinner, w1[:, sl])
    scaled = dnormed * gain_first
    dfirst = rstd1 * (scaled - mean_of(scaled) - hat1 * mean_of(scaled * hat1))
    dfirst_ref[...] = dfirst
    db = dfirst.astype(BF)
    db_ref[...] = db
    datt_ref[...] = dot_nt(db, wo[...]).astype(BF)

    def total(value):
        return jnp.sum(value, axis=0, keepdims=True)

    parts = (db.astype(F32), dnormed * hat1, dnormed, db2.astype(F32), gout * hat2, gout)
    for i, value in enumerate(parts):
        sums_ref[i : i + 1, :] += total(value)


def ffn(at, x_rows, gout, vecs, bias, atts, inner_plan, inner_pieces, outer_plan, outer_pieces, shard):
    rows, width = x_rows.shape
    hidden = bias.shape[1]
    blocks = 4
    tall = rows // blocks

    def row(cols):
        return pl.BlockSpec((tall, cols), lambda i: (i, 0))

    def whole(shape):
        return pl.BlockSpec(shape, lambda i: (0, 0))

    def count(plan, times):
        return times * sum(1 if masks is None else len(masks) for masks, _ in plan)

    shape = jax.ShapeDtypeStruct
    return pl.pallas_call(
        lambda *refs: ffn_kernel((inner_plan, outer_plan, len(atts)), shard, *refs),
        grid=(blocks,),
        in_specs=[SCALAR, row(width), row(width), whole(vecs.shape), whole(bias.shape)]
        + [row(att.shape[1]) for att in atts]
        + [MAT] * (len(inner_pieces) + len(outer_pieces)),
        out_specs=[
            row(width), row(hidden), row(hidden), row(width), row(width), row(width), row(width), row(width),
            whole((8, width)), whole((1, hidden)),
        ],
        out_shape=[
            shape((rows, width), BF), shape((rows, hidden), BF), shape((rows, hidden), BF), shape((rows, width), BF),
            shape((rows, width), BF), shape((rows, width), BF), shape((rows, width), F32), shape((rows, width), BF),
            shape((8, width), F32), shape((1, hidden), F32),
        ],
        scratch_shapes=[
            pltpu.VMEM((width, hidden), BF), pltpu.VMEM((width, width), BF), pltpu.VMEM((hidden, width), BF),
            pltpu.VMEM((tall, hidden), F32), pltpu.SemaphoreType.DMA((count(inner_plan, 2),)),
            pltpu.SemaphoreType.DMA((count(outer_plan, 1),)),
        ],
        compiler_params=pltpu.CompilerParams(vmem_limit_bytes=LIMIT),
        cost_estimate=pl.CostEstimate(
            flops=4 * rows * width * (2 * hidden + width), bytes_accessed=rows * (4 * hidden + 20 * width), transcendentals=2 * rows * hidden
        ),
        name="ffn",
    )(at, x_rows, gout, vecs, bias, *atts, *inner_pieces, *outer_pieces)


def grad_kernel(masks, extra_ref, at_ref, *refs):
    left_ref, rights, (keep_ref, send_ref, done) = refs[0], refs[1:-3], refs[-3:]
    step = pl.program_id(0)
    for number, right in enumerate(rights):
        @pl.when(step == number)
        def _(right=right):
            done[...] = dot_tn(left_ref[...], right[...]).astype(BF)

    size = done.shape[0] // len(masks)
    half = size // 2
    owner, core = at_ref[0], at_ref[1] & 1
    for i, mask in enumerate(masks):
        base = (owner ^ mask) * size
        keep_ref[i, :half] = done[pl.ds(pl.multiple_of(base + core * half, 16), half), :]
        send_ref[i, :half] = done[pl.ds(pl.multiple_of(base + (1 - core) * half, 16), half), :]
        if extra_ref is not None:
            more = jnp.where(step == 0, extra_ref[owner ^ mask], jnp.zeros((), BF))
            keep_ref[i, half:] = more
            send_ref[i, half:] = more


def grad_wide(at, masks, left, rights, extra=None):
    rows, width = left.shape
    steps = len(rights)
    chunk = rights[0].shape[1]
    lines_out = width // len(masks) // 2 + (0 if extra is None else extra.shape[1])
    whole = [pl.BlockSpec((rows, width), lambda i: (0, 0))] + [pl.BlockSpec((rows, chunk), lambda i: (0, 0))] * steps
    extras = [] if extra is None else [extra]
    extra_specs = [pl.BlockSpec(value.shape, lambda i: (0, 0, 0)) for value in extras]
    out = jax.ShapeDtypeStruct((len(masks), lines_out, steps * chunk), BF)
    spec = pl.BlockSpec((len(masks), lines_out, chunk), lambda i: (0, 0, i))

    def kernel(at_ref, *refs):
        if extra is None:
            grad_kernel(masks, None, at_ref, *refs)
        else:
            grad_kernel(masks, refs[0], at_ref, *refs[1:])

    return pl.pallas_call(
        kernel,
        grid=(steps,),
        in_specs=[SCALAR] + extra_specs + whole,
        out_specs=[spec, spec],
        out_shape=[out, out],
        scratch_shapes=[pltpu.VMEM((width, chunk), BF)],
        compiler_params=pltpu.CompilerParams(vmem_limit_bytes=LIMIT),
        cost_estimate=pl.CostEstimate(flops=2 * rows * width * steps * chunk, bytes_accessed=2 * steps * chunk * (rows + width), transcendentals=0),
        name="grad_wide",
    )(at, *extras, left, *rights)


def grad_inner_kernel(masks, at_ref, low_ref, din_ref, att_refs, db_ref, outs, done):
    step = pl.program_id(0)
    last = pl.num_programs(0) - 1
    size = done.shape[0] // len(masks)
    half = size // 2
    wide = done.shape[1] // 2

    @pl.when(step < last)
    def _():
        done[...] = dot_tn(low_ref[...], din_ref[...]).astype(BF)

    @pl.when(step == last)
    def _():
        cols = att_refs[0].shape[1]
        for i, att in enumerate(att_refs):
            done[i * cols : (i + 1) * cols, :] = dot_tn(att[...], db_ref[...]).astype(BF)

    owner, core, side = at_ref[0], at_ref[1] & 1, at_ref[1] >> 1
    for i, mask in enumerate(masks):
        base = (owner ^ mask) * size
        for j, (other_core, other_side) in enumerate(((0, 0), (0, 1), (1, 0), (1, 1))):
            line = pl.multiple_of(base + (core ^ other_core) * half, 16)
            column = pl.multiple_of((side ^ other_side) * wide, 128)
            outs[j][i] = done[pl.ds(line, half), pl.ds(column, wide)]


def grad_inner(at, masks, low, dinner, atts, db):
    rows, width = low.shape
    hidden = dinner.shape[1]
    chunk = width
    steps = hidden // chunk + 1
    size = width // len(masks)
    whole = pl.BlockSpec((rows, width), lambda i: (0, 0))
    out = jax.ShapeDtypeStruct((len(masks), size // 2, steps * chunk // 2), BF)
    spec = pl.BlockSpec((len(masks), size // 2, chunk // 2), lambda i: (0, 0, i))
    n = len(atts)
    return pl.pallas_call(
        lambda at_ref, low_ref, din_ref, *refs: grad_inner_kernel(
            masks, at_ref, low_ref, din_ref, refs[:n], refs[n], refs[n + 1 : n + 5], refs[n + 5]
        ),
        grid=(steps,),
        in_specs=[SCALAR, whole, pl.BlockSpec((rows, chunk), lambda i: (0, jnp.minimum(i, steps - 2)))]
        + [pl.BlockSpec((rows, att.shape[1]), lambda i: (0, 0)) for att in atts]
        + [whole],
        out_specs=[spec] * 4,
        out_shape=[out] * 4,
        scratch_shapes=[pltpu.VMEM((width, chunk), BF)],
        compiler_params=pltpu.CompilerParams(vmem_limit_bytes=LIMIT),
        cost_estimate=pl.CostEstimate(flops=2 * rows * width * (hidden + width), bytes_accessed=4 * rows * hidden, transcendentals=0),
        name="grad_inner",
    )(at, low, dinner, *atts, db)


def grad_outer_kernel(half, at_ref, act_ref, db2_ref, keep_ref, send_ref, done):
    core = at_ref[1] & 1
    done[...] = dot_tn(act_ref[...], db2_ref[...]).astype(BF)
    keep_ref[0] = done[pl.ds(pl.multiple_of(core * half, 16), half), :]
    send_ref[0] = done[pl.ds(pl.multiple_of((1 - core) * half, 16), half), :]


def grad_outer(at, owners, act, db2):
    rows, hidden = act.shape
    width = db2.shape[1]
    size = hidden // owners
    levels = owners.bit_length() - 1

    def column(i, at_ref):
        mask = 0
        for level in range(levels):
            mask = mask | (((i >> level) & 1) << (levels - 1 - level))
        return (0, at_ref[0] ^ mask)

    out = jax.ShapeDtypeStruct((owners, size // 2, width), BF)
    spec = pl.BlockSpec((1, size // 2, width), lambda i, at_ref: (i, 0, 0))
    return pl.pallas_call(
        lambda *refs: grad_outer_kernel(size // 2, *refs),
        grid_spec=pltpu.PrefetchScalarGridSpec(
            num_scalar_prefetch=1,
            grid=(owners,),
            in_specs=[pl.BlockSpec((rows, size), column), pl.BlockSpec((rows, width), lambda i, at_ref: (0, 0))],
            out_specs=[spec, spec],
            scratch_shapes=[pltpu.VMEM((size, width), BF)],
        ),
        out_shape=[out, out],
        compiler_params=pltpu.CompilerParams(vmem_limit_bytes=LIMIT),
        cost_estimate=pl.CostEstimate(flops=2 * rows * width * hidden, bytes_accessed=4 * rows * hidden, transcendentals=0),
        name="grad_outer",
    )(at, act, db2)


def input_kernel(plan, shard, count, at_ref, dfirst_ref, *rest):
    parts, rest = rest[:count], rest[count:]
    pieces, (out_ref, mat, sems) = rest[:-3], rest[-3:]

    @pl.when(pl.program_id(0) == 0)
    def _():
        for copy in load(qkv_copies(plan, pieces, at_ref, mat, shard), sems):
            copy.wait()

    width = mat.shape[0]
    wide = parts[0].shape[1]
    total = dfirst_ref[...]
    for i, part in enumerate(parts):
        start = (i % 3) * width + (i // 3) * wide
        total = total + dot_nt(part[...], mat[:, start : start + wide])
    out_ref[...] = total.astype(BF)


def input_gradient(at, dfirst, parts, plan, pieces, shard):
    rows, width = dfirst.shape
    blocks = 4
    count = sum(1 if masks is None else len(masks) for masks, _ in plan)

    def row(cols):
        return pl.BlockSpec((rows // blocks, cols), lambda i: (i, 0))

    return pl.pallas_call(
        lambda *refs: input_kernel(plan, shard, len(parts), *refs),
        grid=(blocks,),
        in_specs=[SCALAR, row(width)] + [row(part.shape[1]) for part in parts] + [MAT] * len(pieces),
        out_specs=row(width),
        out_shape=jax.ShapeDtypeStruct((rows, width), BF),
        scratch_shapes=[pltpu.VMEM((width, 3 * width), BF), pltpu.SemaphoreType.DMA((count,))],
        compiler_params=pltpu.CompilerParams(vmem_limit_bytes=LIMIT),
        cost_estimate=pl.CostEstimate(flops=6 * rows * width * width, bytes_accessed=14 * rows * width, transcendentals=0),
        name="input_gradient",
    )(at, dfirst, *parts, *pieces)


def column_sum(value):
    return jnp.sum(value.astype(F32), axis=0)


def fold(parts):
    return sum(part.astype(F32) for part in parts)


def halve(parts):
    half = parts[0].shape[0] // 2
    return fold([part[half:] for part in parts]).astype(BF), [part[:half] for part in parts]


def reduce_to_owner(value, owners):
    index = lax.axis_index("fsdp")
    parts = [value]
    for bit in reversed(bits_of(owners)):
        flag = (index // bit) & 1
        pairs = [part.reshape((-1, 2) + part.shape[1:]) for part in parts]
        sent = fold([pick(flag, pair[:, 1], pair[:, 0]) for pair in pairs]).astype(BF)
        parts = [pick(flag, pair[:, 0], pair[:, 1]) for pair in pairs] + [swap(sent, "fsdp", bit)]
    total = fold([part[0] for part in parts])
    for bit in (1, 2):
        own = total.astype(BF)
        total = own.astype(F32) + swap(own, "seq", bit).astype(F32)
    return total


def body(
    tokens, segment_ids, out_cotangent, query_weight, query_bias, key_weight, value_weight, value_bias,
    output_weight, output_bias, attn_gain, attn_shift, inner_weight, inner_bias, outer_weight, outer_bias,
    final_gain, final_shift,
):
    groups = lax.axis_size("seq")
    owners = lax.axis_size("fsdp")
    micro, seq_count, local_len, width = tokens.shape
    assert micro * seq_count == groups == 4
    rows = groups * local_len
    shard = query_weight.shape[0]
    hidden = inner_weight.shape[1]
    wide = hidden // owners
    lots = wide // shard
    aligned = shard % 32 == 0 and owners == 8
    place = lax.axis_index("seq")
    core = place & 1
    at = jnp.stack([lax.axis_index("fsdp"), place]).astype(jnp.int32)
    masks = order_of(owners)

    def to_sequences(value):
        return lax.all_to_all(value.reshape((groups, local_len) + value.shape[3:]), "seq", 0, 0, tiled=True)

    def to_tokens(value):
        moved = lax.all_to_all(value.reshape(groups, local_len, width), "seq", 0, 0, tiled=True)
        return moved.reshape(micro, seq_count, local_len, width)

    small = jnp.stack(
        [query_bias, value_bias, output_bias, attn_gain, attn_shift, outer_bias, final_gain, final_shift]
        + [inner_bias[i * shard : (i + 1) * shard] for i in range(lots)]
    )
    piece_a = pick(
        core,
        jnp.concatenate([query_weight, key_weight[:, : width // 2]], axis=1),
        jnp.concatenate([key_weight[:, width // 2 :], value_weight], axis=1),
    )
    piece_b = pick(
        core,
        jnp.concatenate([inner_weight[:, : hidden // 2], output_weight[:, : width // 2]], axis=1),
        jnp.concatenate([inner_weight[:, hidden // 2 :], output_weight[:, width // 2 :]], axis=1),
    )
    if aligned:
        a_far = swap(piece_a[None], "fsdp", 4)
        small_full = absolute(small[None], owners)
        x_rows = to_sequences(tokens).reshape(rows, width)
        doc = to_sequences(segment_ids).reshape(rows, 1)
        a_low = jnp.concatenate([piece_a[None], a_far])
        a_two = swap(a_low, "fsdp", 2)
        a_one = swap(a_low, "fsdp", 1)
        quarter = wide // 4
        piece_c = lax.dynamic_slice(outer_weight, (place * quarter, 0), (quarter, width))[None]
        c_far = swap(after(piece_c, a_two), "fsdp", 4)
        a_three = swap(a_two, "fsdp", 1)
        a_mine = [a_low, a_two, a_one, a_three]
        a_other = [swap(value, "seq", 1) for value in a_mine]
        quads = [(0, 4), (2, 6), (1, 5), (3, 7)]
        plan_a = [(quad, 0) for quad in quads] + [(quad, 1) for quad in quads]
        pieces_a = a_mine + a_other
    else:
        small_full = absolute(small[None], owners)
        x_rows = to_sequences(tokens).reshape(rows, width)
        doc = to_sequences(segment_ids).reshape(rows, 1)
        mine = absolute(piece_a[None], owners).reshape(width, -1)
        plan_a = [(None, 0), (None, 1)]
        pieces_a = [mine, swap(mine, "seq", 1)]
    small_full = small_full.astype(F32)
    vecs = small_full[:, :8].transpose(1, 0, 2).reshape(8, width)
    inner_vec = small_full[:, 8:].reshape(1, hidden)
    qkv_vec = jnp.concatenate([vecs[0:1], jnp.zeros((1, width), F32), vecs[1:2]], axis=1)
    ffn_vecs = vecs[2:]

    if aligned:
        qkv = project(at, after(x_rows, c_far), qkv_vec, plan_a, pieces_a, shard)
    else:
        qkv = project(at, x_rows, qkv_vec, plan_a, pieces_a, shard)
    pairs = width // PAIR
    calls = 3
    each = pairs // calls
    atts, logs = [], []
    if aligned:
        c_low = jnp.concatenate([piece_c, c_far])
        c_two = swap(c_low, "fsdp", 2)
        c_one = swap(c_low, "fsdp", 1)
        b_far = swap(after(piece_b, c_far)[None], "fsdp", 4)
        qkv = after(qkv, c_two, c_one)
        att, log = attend(doc, qkv, 0, each)
        atts.append(att)
        logs.append(log)
        c_three = swap(c_two, "fsdp", 1)
        c_side = [swap(c_low, "seq", 2), swap(c_two, "seq", 2)]
        b_low = jnp.concatenate([piece_b[None], b_far])
        qkv, _ = lax.optimization_barrier((qkv, (att, b_low, c_three, c_side)))
        att, log = attend(doc, qkv, each, each)
        atts.append(att)
        logs.append(log)
        b_two = swap(b_low, "fsdp", 2)
        b_one = swap(b_low, "fsdp", 1)
        c_side += [swap(c_one, "seq", 2), swap(c_three, "seq", 2)]
        grads_in = to_sequences(out_cotangent).reshape(rows, width)
        qkv, _ = lax.optimization_barrier((qkv, (att, b_two, b_one, c_side)))
        att, log = attend(doc, qkv, 2 * each, each)
        atts.append(att)
        logs.append(log)
        b_three = swap(b_two, "fsdp", 1)
        b_mine = [b_low, b_two, b_one, b_three]
        b_other = [swap(value, "seq", 1) for value in b_mine]
        plan_b, pieces_b = plan_a, b_mine + b_other
        c_mine = [c_low, c_two, c_one, c_three]
        c_all = c_mine + c_side
        plan_c = [(quad, mask) for mask in (0, 2, 1, 3) for quad in quads]
        pieces_c = c_all + [swap(value, "seq", 1) for value in c_all]
    else:
        for call in range(calls):
            att, log = attend(doc, qkv, call * each, each)
            atts.append(att)
            logs.append(log)
        grads_in = to_sequences(out_cotangent).reshape(rows, width)
        mine = absolute(piece_b[None], owners).reshape(width, -1)
        plan_b, pieces_b = plan_a, [mine, swap(mine, "seq", 1)]
        plan_c, pieces_c = [(None, 0)], [absolute(outer_weight[None], owners).reshape(hidden, width)]
    result, active, dinner, low, db2, db, dfirst, dattended, sums, dinner_vec = ffn(
        at, x_rows, grads_in, ffn_vecs, inner_vec, atts, plan_b, pieces_b, plan_c, pieces_c, shard
    )
    backs = []

    def back(call, gate):
        return attend_back(doc, qkv, atts[call], gate, logs[call], call * each, each)

    def vectors():
        dq = jnp.concatenate([one[3] for one in backs], axis=1)
        dv = jnp.concatenate([one[4] for one in backs], axis=1)
        eight = jnp.concatenate([dq, dv, sums[:6]]).reshape(8, owners, shard).transpose(1, 0, 2)
        return jnp.concatenate([eight, dinner_vec.reshape(owners, lots, shard)], axis=1)

    if aligned:
        outer_keep, outer_send = grad_outer(at, owners, active, db2)
        outer_parts = [outer_keep, swap(outer_send, "seq", 1)]
        inner_kept, inner_side, inner_core, inner_both = grad_inner(at, masks, after(low, outer_keep), dinner, atts, db)
        outer_x, outer_parts = halve(outer_parts)
        gate = after(dattended, inner_kept, outer_x)
        backs.append(back(0, gate))
        outer_parts.append(swap(outer_x, "fsdp", 1))
        inner_parts = [inner_kept, swap(inner_core, "seq", 1)]
        inner_y = fold([inner_side, swap(inner_both, "seq", 1)]).astype(BF)
        gate, shown, _ = lax.optimization_barrier((gate, result, (backs[0], inner_y, inner_parts)))
        layer_out = to_tokens(shown)
        backs.append(back(1, gate))
        inner_parts.append(swap(inner_y, "seq", 2))
        both = [jnp.concatenate([one[j] for one in backs], axis=1) for j in range(3)]
        first_keep, first_send = grad_wide(at, masks, x_rows, both)
        outer_z, outer_parts = halve(outer_parts)
        gate, layer_out, _ = lax.optimization_barrier((gate, layer_out, (first_keep, outer_z)))
        backs.append(back(2, gate))
        outer_parts.append(swap(outer_z, "fsdp", 2))
        first_parts = [first_keep, swap(first_send, "seq", 1)]
        outer_zz, outer_parts = halve(outer_parts)
        inner_x, inner_parts = halve(inner_parts)
        first_x, first_parts = halve(first_parts)
        extra = vectors()
        extra = jnp.pad(extra, ((0, 0), (0, 16 - extra.shape[1]), (0, each * PAIR - shard))).astype(BF)
        gated, _ = lax.optimization_barrier((x_rows, (outer_zz, inner_x, first_x)))
        second_keep, second_send = grad_wide(at, masks, gated, backs[2][:3], extra)
        dfirst, _ = lax.optimization_barrier((dfirst, (second_keep,)))
        parts = [value for one in backs for value in one[:3]]
        moved = input_gradient(at, dfirst, parts, plan_a, pieces_a, shard)
        input_grad = to_tokens(moved).astype(F32)
        outer_parts.append(swap(outer_zz, "fsdp", 4))
        inner_parts.append(swap(inner_x, "fsdp", 1))
        first_parts.append(swap(first_x, "fsdp", 1))
        second_parts = [second_keep, swap(second_send, "seq", 1)]
        second_x, second_parts = halve(second_parts)
        second_parts.append(swap(second_x, "fsdp", 1))
        groups_left = [inner_parts, first_parts, second_parts]
        for bit in (2, 4):
            sends = [halve(group) for group in groups_left]
            groups_left = [keep + [swap(sent, "fsdp", bit)] for sent, keep in sends]
        owns = [fold([part[0] for part in group]).astype(BF) for group in [outer_parts] + groups_left]
        others = [swap(own, "seq", 2) for own in owns]
        outer_own, first_own, second_own = (
            owns[i].astype(F32) + others[i].astype(F32) for i in (0, 2, 3)
        )
        side = place >> 1
        half = shard // 2
        cols = width // 2
        inner_own = pick(
            side,
            jnp.stack([value.reshape(half, -1, cols) for value in (owns[1], others[1])], axis=2),
            jnp.stack([value.reshape(half, -1, cols) for value in (others[1], owns[1])], axis=2),
        ).reshape(half, hidden + width)

        def whole(own):
            other = swap(own, "seq", 1)
            return pick(core, jnp.concatenate([own, other]), jnp.concatenate([other, own])).astype(F32)

        douter = whole(outer_own)
        dinner_full = whole(inner_own)
        part = 2 * each * PAIR
        firsts = whole(first_own)
        seconds = whole(second_own[:half])
        rest = each * PAIR
        dqkv = [
            jnp.concatenate([firsts[:, i * part : (i + 1) * part], seconds[:, i * rest : (i + 1) * rest]], axis=1)
            for i in range(3)
        ]
        vec = second_own[half : half + 8 + lots, :shard]
        dinner_w, doutput = dinner_full[:, :hidden], dinner_full[:, hidden:]
    else:
        for call in range(calls):
            backs.append(back(call, dattended))
        parts = [value for one in backs for value in one[:3]]
        moved = input_gradient(at, dfirst, parts, plan_a, pieces_a, shard)
        input_grad = to_tokens(moved).astype(F32)
        layer_out = to_tokens(result)
        three = [jnp.concatenate([one[j] for one in backs], axis=1) for j in range(3)]
        att = jnp.concatenate(atts, axis=1)
        lefts = [x_rows, x_rows, x_rows, att, low]
        rights = three + [db, dinner]
        dqkv = []
        for left, right in zip(lefts, rights):
            dqkv.append(reduce_to_owner(dot_tn(left, right).astype(BF).reshape(owners, shard, -1), owners))
        doutput, dinner_w = dqkv[3:]
        douter = reduce_to_owner(dot_tn(active, db2).astype(BF).reshape(owners, wide, width), owners)
        vec = reduce_to_owner(vectors().astype(BF), owners)
    return (
        layer_out, input_grad, dqkv[0], vec[0], dqkv[1], dqkv[2], vec[1], doutput, vec[2], vec[3], vec[4], dinner_w,
        vec[8:].reshape(wide), douter, vec[5], vec[6], vec[7],
    )


def solution(mesh):
    rows = P(None, "fsdp", "seq", None)
    mat = P("fsdp", None)
    vec = P("fsdp")
    return jax.shard_map(
        body,
        mesh=mesh,
        in_specs=(
            rows, P(None, "fsdp", "seq"), rows, mat, vec, mat, mat, vec, mat, vec, vec, vec, mat, vec, mat, vec, vec, vec,
        ),
        out_specs=(rows, rows, mat, vec, mat, mat, vec, mat, vec, vec, vec, mat, vec, mat, vec, vec, vec),
        check_vma=False,
    )
```

```python
import math

import jax
import jax.numpy as jnp
from jax import lax
from jax.experimental import pallas as pl
from jax.experimental.pallas import tpu as pltpu
from jax.sharding import PartitionSpec as P

F32=jnp.float32; BF=jnp.bfloat16
PAIR=128; HD=64; BIG=1e30

def dot_nn(a,b): return lax.dot_general(a,b,(((1,),(0,)),((),())),preferred_element_type=F32)
def dot_nt(a,b): return lax.dot_general(a,b,(((1,),(1,)),((),())),preferred_element_type=F32)
def dot_tn(a,b): return lax.dot_general(a,b,(((0,),(0,)),((),())),preferred_element_type=F32)

def split3(v):
    hi=v.astype(BF); r=v-hi.astype(F32); mid=r.astype(BF); lo=(r-mid.astype(F32)).astype(BF)
    return hi,mid,lo

def fwd_kernel(doc_ref,q_ref,k_ref,v_ref,o_ref,lse_ref,qa,ka,va):
    rows=q_ref.shape[0]
    lane=lax.broadcasted_iota(jnp.int32,(rows,PAIR),1)
    doc=doc_ref[...]
    for h in range(2):
        base=(1-h)*HD
        mine=(lane>=h*HD)&(lane<(h+1)*HD)
        same=(lane-base)==doc
        qa[...]=jnp.where(mine,q_ref[...]*jnp.asarray(0.125,BF),jnp.where(same,1.0,0.0).astype(BF))
        ka[...]=jnp.where(mine,k_ref[...],jnp.where(same|(lane<base)|(lane>=base+8),0.0,-BIG).astype(BF))
        va[...]=jnp.where(mine,v_ref[...],jnp.ones((),BF))
        bq=256
        for i in range(rows//bq):
            sl=slice(i*bq,(i+1)*bq)
            sc=dot_nt(qa[sl,:],ka[...])
            m=jnp.max(sc,axis=1,keepdims=True)
            p=jnp.exp(sc-m).astype(BF)
            o=dot_nn(p,va[...])
            l=o[:,base:base+1]
            lse_ref[sl,h:h+1]=m+jnp.log(l)
            out=(o/l).astype(BF)
            if h==0: o_ref[sl,:]=out
            else: o_ref[sl,:]=jnp.where(lane[sl,:]>=HD,out,o_ref[sl,:])

def attend(doc,qkv,first,n):
    rows=qkv.shape[0]; pairs=qkv.shape[1]//3//PAIR
    return pl.pallas_call(fwd_kernel,grid=(n,),
        in_specs=[pl.BlockSpec((rows,1),lambda h:(0,0))]+[pl.BlockSpec((rows,PAIR),lambda h,j=j:(0,h+first+j*pairs)) for j in range(3)],
        out_specs=[pl.BlockSpec((rows,PAIR),lambda h:(0,h)),pl.BlockSpec((None,rows,2),lambda h:(h,0,0))],
        out_shape=[jax.ShapeDtypeStruct((rows,n*PAIR),BF),jax.ShapeDtypeStruct((n,rows,2),F32)],
        scratch_shapes=[pltpu.VMEM((rows,PAIR),BF)]*3,
        compiler_params=pltpu.CompilerParams(vmem_limit_bytes=60<<20),
        cost_estimate=pl.CostEstimate(flops=16*rows*rows*PAIR*n,bytes_accessed=rows*PAIR*n*8,transcendentals=rows*rows*n*2),
        name="attend")(doc,qkv,qkv,qkv)

def bwd_kernel(doc_ref,q_ref,k_ref,v_ref,o_ref,do_ref,lse_ref,dq_ref,dk_ref,dv_ref,dqsum_ref,dvsum_ref,qa,ka,va,da,dqs):
    rows=q_ref.shape[0]
    lane=lax.broadcasted_iota(jnp.int32,(rows,PAIR),1)
    doc=doc_ref[...]
    dof=do_ref[...].astype(F32)*o_ref[...].astype(F32)
    for h in range(2):
        base=(1-h)*HD
        mine=(lane>=h*HD)&(lane<(h+1)*HD)
        rel=lane-base
        same=rel==doc
        delta=jnp.sum(jnp.where(mine,dof,0.0),axis=1,keepdims=True)
        lh,lm,ll=split3(-lse_ref[:,h:h+1]); dh,dm,dl=split3(-delta)
        one=jnp.ones((),BF); zero=jnp.zeros((),BF)
        aug_q=jnp.where(same,one,zero)
        aug_q=jnp.where(rel==8,lh,jnp.where(rel==9,lm,jnp.where(rel==10,ll,aug_q)))
        aug_k=jnp.where((rel>=0)&(rel<8)&(~same),jnp.asarray(-BIG,BF),zero)
        aug_k=jnp.where((rel>=8)&(rel<11),one,aug_k)
        aug_d=jnp.where(rel==8,dh,jnp.where(rel==9,dm,jnp.where(rel==10,dl,zero)))
        aug_v=jnp.where((rel>=8)&(rel<11),one,zero)
        qa[...]=jnp.where(mine,q_ref[...]*jnp.asarray(0.125,BF),aug_q)
        ka[...]=jnp.where(mine,k_ref[...],aug_k)
        va[...]=jnp.where(mine,v_ref[...],aug_v)
        da[...]=jnp.where(mine,do_ref[...],aug_d)
        bk=256
        for i in range(rows//bk):
            sl=slice(i*bk,(i+1)*bk)
            st=dot_nt(ka[sl,:],qa[...])
            pt=jnp.exp(st)
            dpt=dot_nt(va[sl,:],da[...])
            dst=(pt*dpt).astype(BF)
            dv=dot_nn(pt.astype(BF),da[...])
            dk=dot_nn(dst,qa[...])
            dq=dot_tn(dst,ka[sl,:])
            if i==0: dqs[...]=dq
            else: dqs[...]+=dq
            msl=mine[sl,:]
            if h==0:
                dv_ref[sl,:]=dv.astype(BF); dk_ref[sl,:]=dk.astype(BF)
            else:
                dv_ref[sl,:]=jnp.where(msl,dv.astype(BF),dv_ref[sl,:]); dk_ref[sl,:]=jnp.where(msl,dk.astype(BF),dk_ref[sl,:])
        dqv=(dqs[...]*0.125).astype(BF)
        if h==0: dq_ref[...]=dqv
        else: dq_ref[...]=jnp.where(mine,dqv,dq_ref[...])
    dqsum_ref[...]=jnp.sum(dq_ref[...].astype(F32),axis=0,keepdims=True)
    dvsum_ref[...]=jnp.sum(dv_ref[...].astype(F32),axis=0,keepdims=True)

def attend_back(doc,qkv,att,datt,lse,first,n):
    rows=qkv.shape[0]; pairs=qkv.shape[1]//3//PAIR
    col=lambda h:(0,h+first)
    return pl.pallas_call(bwd_kernel,grid=(n,),
        in_specs=[pl.BlockSpec((rows,1),lambda h:(0,0))]+[pl.BlockSpec((rows,PAIR),lambda h,j=j:(0,h+first+j*pairs)) for j in range(3)]
          +[pl.BlockSpec((rows,PAIR),lambda h:(0,h)),pl.BlockSpec((rows,PAIR),col),pl.BlockSpec((None,rows,2),lambda h:(h,0,0))],
        out_specs=[pl.BlockSpec((rows,PAIR),lambda h:(0,h))]*3+[pl.BlockSpec((1,PAIR),lambda h:(0,h))]*2,
        out_shape=[jax.ShapeDtypeStruct((rows,n*PAIR),BF)]*3+[jax.ShapeDtypeStruct((1,n*PAIR),F32)]*2,
        scratch_shapes=[pltpu.VMEM((rows,PAIR),BF)]*4+[pltpu.VMEM((rows,PAIR),F32)],
        compiler_params=pltpu.CompilerParams(vmem_limit_bytes=60<<20),
        cost_estimate=pl.CostEstimate(flops=24*rows*rows*PAIR*n,bytes_accessed=rows*PAIR*n*16,transcendentals=rows*rows*n*2),
        name="attend_back")(doc,qkv,qkv,qkv,att,datt,lse)

norm_eps = 1e-12
MAT = pl.BlockSpec(memory_space=pl.ANY)
SCALAR = pl.BlockSpec(memory_space=pltpu.SMEM)
LIMIT = 60 << 20


def swap(value, axis, mask):
    size = lax.axis_size(axis)
    return lax.ppermute(value, axis, [(i, i ^ mask) for i in range(size)])


def after(value, *deps):
    return lax.optimization_barrier((value,) + deps)[0]


def pick(flag, low, high):
    return jnp.where(flag == 0, low, high)


def bits_of(count):
    return [1 << i for i in reversed(range(count.bit_length() - 1))]


def order_of(owners):
    masks = [0]
    for bit in bits_of(owners):
        masks = masks + [m ^ bit for m in masks]
    return masks


def absolute(held, owners):
    index = lax.axis_index("fsdp")
    for bit in bits_of(owners):
        other = swap(held, "fsdp", bit)
        flag = (index // bit) & 1
        held = pick(flag, jnp.stack([held, other], axis=1), jnp.stack([other, held], axis=1))
        held = held.reshape((-1,) + held.shape[2:])
    return held


def load(copies, sems):
    started = [pltpu.make_async_copy(src, dst, sems.at[i]) for i, (src, dst) in enumerate(copies)]
    for copy in started:
        copy.start()
    return started


def piece_copies(plan, refs, at_ref, place):
    owner, part = at_ref[0], at_ref[1]
    copies = []
    for (masks, seq_mask), ref in zip(plan, refs):
        if masks is None:
            copies += place(ref, None, part ^ seq_mask)
        else:
            for i, mask in enumerate(masks):
                copies += place(ref.at[i], owner ^ mask, part ^ seq_mask)
    return copies


def project_kernel(plan, shard, at_ref, x_ref, bias_ref, *rest):
    pieces, (out_ref, mat, sems) = rest[:-3], rest[-3:]
    half = mat.shape[1] // 2

    @pl.when(pl.program_id(0) == 0)
    def _():
        for copy in load(qkv_copies(plan, pieces, at_ref, mat, shard), sems):
            copy.wait()

    out_ref[...] = (dot_nn(x_ref[...], mat[...]) + bias_ref[...]).astype(BF)


def columns(part, size):
    return pl.ds(pl.multiple_of(part * size, 128), size)


def lines(owner, size):
    return pl.ds(pl.multiple_of(owner * size, 16), size)


def qkv_copies(plan, refs, at_ref, mat, shard):
    half = mat.shape[1] // 2

    def place(src, owner, part):
        if owner is None:
            return [(src, mat.at[:, columns(part & 1, half)])]
        return [(src, mat.at[lines(owner, shard), columns(part & 1, half)])]

    return piece_copies(plan, refs, at_ref, place)


def project(at, x_rows, bias, plan, pieces, shard):
    rows, width = x_rows.shape
    blocks = 4
    count = sum(1 if masks is None else len(masks) for masks, _ in plan)
    return pl.pallas_call(
        lambda *refs: project_kernel(plan, shard, *refs),
        grid=(blocks,),
        in_specs=[SCALAR, pl.BlockSpec((rows // blocks, width), lambda i: (i, 0)), pl.BlockSpec((1, 3 * width), lambda i: (0, 0))]
        + [MAT] * len(pieces),
        out_specs=pl.BlockSpec((rows // blocks, 3 * width), lambda i: (i, 0)),
        out_shape=jax.ShapeDtypeStruct((rows, 3 * width), BF),
        scratch_shapes=[pltpu.VMEM((width, 3 * width), BF), pltpu.SemaphoreType.DMA((count,))],
        compiler_params=pltpu.CompilerParams(vmem_limit_bytes=LIMIT),
        cost_estimate=pl.CostEstimate(flops=6 * rows * width * width, bytes_accessed=14 * rows * width, transcendentals=0),
        name="project",
    )(at, x_rows, bias, *pieces)


def mean_of(value):
    return jnp.mean(value, axis=-1, keepdims=True)


def ffn_kernel(plans, shard, at_ref, x_ref, gout_ref, vec_ref, bias_ref, *rest):
    count_att = plans[2]
    atts, rest = rest[:count_att], rest[count_att:]
    inner_pieces, rest = rest[: len(plans[0])], rest[len(plans[0]) :]
    outer_pieces, rest = rest[: len(plans[1])], rest[len(plans[1]) :]
    (
        res_ref, act_ref, din_ref, low_ref, db2_ref, db_ref, dfirst_ref, datt_ref, sums_ref, dsum_ref,
        w1, wo, w2, slope, sem_a, sem_b,
    ) = rest
    width, hidden = w1.shape
    step = pl.program_id(0)

    @pl.when(step == 0)
    def _():
        def place(src, owner, part):
            if owner is None:
                rows = slice(None)
            else:
                rows = lines(owner, shard)
            part = part & 1
            return [
                (src.at[:, : hidden // 2], w1.at[rows, columns(part, hidden // 2)]),
                (src.at[:, hidden // 2 :], wo.at[rows, columns(part, width // 2)]),
            ]

        def place_outer(src, owner, part):
            if owner is None:
                return [(src, w2)]
            size = src.shape[0]
            return [(src, w2.at[lines(owner * 4 + part, size)])]

        first = load(piece_copies(plans[0], inner_pieces, at_ref, place), sem_a)
        later = load(piece_copies(plans[1], outer_pieces, at_ref, place_outer), sem_b)
        for copy in first + later:
            copy.wait()
        sums_ref[...] = jnp.zeros_like(sums_ref)
        dsum_ref[...] = jnp.zeros_like(dsum_ref)

    output_vec, gain_first, shift_first, outer_vec, gain_final, shift_final = (
        vec_ref[i : i + 1, :] for i in range(6)
    )
    wide = atts[0].shape[1]
    first = x_ref[...].astype(F32) + output_vec
    for i, att in enumerate(atts):
        first = first + dot_nn(att[...], wo[i * wide : (i + 1) * wide, :])
    center = first - mean_of(first)
    rstd1 = lax.rsqrt(mean_of(center * center) + norm_eps)
    hat1 = center * rstd1
    normed = hat1 * gain_first + shift_first
    low = normed.astype(BF)
    low_ref[...] = low
    chunk = 768
    second = normed + outer_vec
    for start in range(0, hidden, chunk):
        sl = slice(start, start + chunk)
        inner = dot_nn(low, w1[:, sl]) + bias_ref[:, sl]
        cdf = 0.5 * (1.0 + lax.erf(inner * (1.0 / math.sqrt(2.0))))
        act = (inner * cdf).astype(BF)
        slope[:, sl] = cdf + inner * (jnp.exp(-0.5 * inner * inner) * (1.0 / math.sqrt(2.0 * math.pi)))
        act_ref[:, sl] = act
        second = second + dot_nn(act, w2[sl, :])
    center = second - mean_of(second)
    rstd2 = lax.rsqrt(mean_of(center * center) + norm_eps)
    hat2 = center * rstd2
    res_ref[...] = (hat2 * gain_final + shift_final).astype(BF)
    gout = gout_ref[...].astype(F32)
    scaled = gout * gain_final
    dsecond = rstd2 * (scaled - mean_of(scaled) - hat2 * mean_of(scaled * hat2))
    db2 = dsecond.astype(BF)
    db2_ref[...] = db2
    dnormed = dsecond
    for start in range(0, hidden, chunk):
        sl = slice(start, start + chunk)
        dinner = (dot_nt(db2, w2[sl, :]) * slope[:, sl]).astype(BF)
        din_ref[:, sl] = dinner
        dsum_ref[:, sl] += jnp.sum(dinner.astype(F32), axis=0, keepdims=True)
        dnormed = dnormed + dot_nt(dinner, w1[:, sl])
    scaled = dnormed * gain_first
    dfirst = rstd1 * (scaled - mean_of(scaled) - hat1 * mean_of(scaled * hat1))
    dfirst_ref[...] = dfirst
    db = dfirst.astype(BF)
    db_ref[...] = db
    datt_ref[...] = dot_nt(db, wo[...]).astype(BF)

    def total(value):
        return jnp.sum(value, axis=0, keepdims=True)

    parts = (db.astype(F32), dnormed * hat1, dnormed, db2.astype(F32), gout * hat2, gout)
    for i, value in enumerate(parts):
        sums_ref[i : i + 1, :] += total(value)


def ffn(at, x_rows, gout, vecs, bias, atts, inner_plan, inner_pieces, outer_plan, outer_pieces, shard):
    rows, width = x_rows.shape
    hidden = bias.shape[1]
    blocks = 4
    tall = rows // blocks

    def row(cols):
        return pl.BlockSpec((tall, cols), lambda i: (i, 0))

    def whole(shape):
        return pl.BlockSpec(shape, lambda i: (0, 0))

    def count(plan, times):
        return times * sum(1 if masks is None else len(masks) for masks, _ in plan)

    shape = jax.ShapeDtypeStruct
    return pl.pallas_call(
        lambda *refs: ffn_kernel((inner_plan, outer_plan, len(atts)), shard, *refs),
        grid=(blocks,),
        in_specs=[SCALAR, row(width), row(width), whole(vecs.shape), whole(bias.shape)]
        + [row(att.shape[1]) for att in atts]
        + [MAT] * (len(inner_pieces) + len(outer_pieces)),
        out_specs=[
            row(width), row(hidden), row(hidden), row(width), row(width), row(width), row(width), row(width),
            whole((8, width)), whole((1, hidden)),
        ],
        out_shape=[
            shape((rows, width), BF), shape((rows, hidden), BF), shape((rows, hidden), BF), shape((rows, width), BF),
            shape((rows, width), BF), shape((rows, width), BF), shape((rows, width), F32), shape((rows, width), BF),
            shape((8, width), F32), shape((1, hidden), F32),
        ],
        scratch_shapes=[
            pltpu.VMEM((width, hidden), BF), pltpu.VMEM((width, width), BF), pltpu.VMEM((hidden, width), BF),
            pltpu.VMEM((tall, hidden), F32), pltpu.SemaphoreType.DMA((count(inner_plan, 2),)),
            pltpu.SemaphoreType.DMA((count(outer_plan, 1),)),
        ],
        compiler_params=pltpu.CompilerParams(vmem_limit_bytes=LIMIT),
        cost_estimate=pl.CostEstimate(
            flops=4 * rows * width * (2 * hidden + width), bytes_accessed=rows * (4 * hidden + 20 * width), transcendentals=2 * rows * hidden
        ),
        name="ffn",
    )(at, x_rows, gout, vecs, bias, *atts, *inner_pieces, *outer_pieces)


def grad_kernel(masks, extra_ref, at_ref, *refs):
    left_ref, rights, (keep_ref, send_ref, done) = refs[0], refs[1:-3], refs[-3:]
    step = pl.program_id(0)
    for number, right in enumerate(rights):
        @pl.when(step == number)
        def _(right=right):
            done[...] = dot_tn(left_ref[...], right[...]).astype(BF)

    size = done.shape[0] // len(masks)
    half = size // 2
    owner, core = at_ref[0], at_ref[1] & 1
    for i, mask in enumerate(masks):
        base = (owner ^ mask) * size
        keep_ref[i, :half] = done[pl.ds(pl.multiple_of(base + core * half, 16), half), :]
        send_ref[i, :half] = done[pl.ds(pl.multiple_of(base + (1 - core) * half, 16), half), :]
        if extra_ref is not None:
            more = jnp.where(step == 0, extra_ref[owner ^ mask], jnp.zeros((), BF))
            keep_ref[i, half:] = more
            send_ref[i, half:] = more


def grad_wide(at, masks, left, rights, extra=None):
    rows, width = left.shape
    steps = len(rights)
    chunk = rights[0].shape[1]
    lines_out = width // len(masks) // 2 + (0 if extra is None else extra.shape[1])
    whole = [pl.BlockSpec((rows, width), lambda i: (0, 0))] + [pl.BlockSpec((rows, chunk), lambda i: (0, 0))] * steps
    extras = [] if extra is None else [extra]
    extra_specs = [pl.BlockSpec(value.shape, lambda i: (0, 0, 0)) for value in extras]
    out = jax.ShapeDtypeStruct((len(masks), lines_out, steps * chunk), BF)
    spec = pl.BlockSpec((len(masks), lines_out, chunk), lambda i: (0, 0, i))

    def kernel(at_ref, *refs):
        if extra is None:
            grad_kernel(masks, None, at_ref, *refs)
        else:
            grad_kernel(masks, refs[0], at_ref, *refs[1:])

    return pl.pallas_call(
        kernel,
        grid=(steps,),
        in_specs=[SCALAR] + extra_specs + whole,
        out_specs=[spec, spec],
        out_shape=[out, out],
        scratch_shapes=[pltpu.VMEM((width, chunk), BF)],
        compiler_params=pltpu.CompilerParams(vmem_limit_bytes=LIMIT),
        cost_estimate=pl.CostEstimate(flops=2 * rows * width * steps * chunk, bytes_accessed=2 * steps * chunk * (rows + width), transcendentals=0),
        name="grad_wide",
    )(at, *extras, left, *rights)


def grad_inner_kernel(masks, at_ref, low_ref, din_ref, att_refs, db_ref, outs, done):
    step = pl.program_id(0)
    last = pl.num_programs(0) - 1
    size = done.shape[0] // len(masks)
    half = size // 2
    wide = done.shape[1] // 2

    @pl.when(step < last)
    def _():
        done[...] = dot_tn(low_ref[...], din_ref[...]).astype(BF)

    @pl.when(step == last)
    def _():
        cols = att_refs[0].shape[1]
        for i, att in enumerate(att_refs):
            done[i * cols : (i + 1) * cols, :] = dot_tn(att[...], db_ref[...]).astype(BF)

    owner, core, side = at_ref[0], at_ref[1] & 1, at_ref[1] >> 1
    for i, mask in enumerate(masks):
        base = (owner ^ mask) * size
        for j, (other_core, other_side) in enumerate(((0, 0), (0, 1), (1, 0), (1, 1))):
            line = pl.multiple_of(base + (core ^ other_core) * half, 16)
            column = pl.multiple_of((side ^ other_side) * wide, 128)
            outs[j][i] = done[pl.ds(line, half), pl.ds(column, wide)]


def grad_inner(at, masks, low, dinner, atts, db):
    rows, width = low.shape
    hidden = dinner.shape[1]
    chunk = width
    steps = hidden // chunk + 1
    size = width // len(masks)
    whole = pl.BlockSpec((rows, width), lambda i: (0, 0))
    out = jax.ShapeDtypeStruct((len(masks), size // 2, steps * chunk // 2), BF)
    spec = pl.BlockSpec((len(masks), size // 2, chunk // 2), lambda i: (0, 0, i))
    n = len(atts)
    return pl.pallas_call(
        lambda at_ref, low_ref, din_ref, *refs: grad_inner_kernel(
            masks, at_ref, low_ref, din_ref, refs[:n], refs[n], refs[n + 1 : n + 5], refs[n + 5]
        ),
        grid=(steps,),
        in_specs=[SCALAR, whole, pl.BlockSpec((rows, chunk), lambda i: (0, jnp.minimum(i, steps - 2)))]
        + [pl.BlockSpec((rows, att.shape[1]), lambda i: (0, 0)) for att in atts]
        + [whole],
        out_specs=[spec] * 4,
        out_shape=[out] * 4,
        scratch_shapes=[pltpu.VMEM((width, chunk), BF)],
        compiler_params=pltpu.CompilerParams(vmem_limit_bytes=LIMIT),
        cost_estimate=pl.CostEstimate(flops=2 * rows * width * (hidden + width), bytes_accessed=4 * rows * hidden, transcendentals=0),
        name="grad_inner",
    )(at, low, dinner, *atts, db)


def grad_outer_kernel(half, at_ref, act_ref, db2_ref, keep_ref, send_ref, done):
    core = at_ref[1] & 1
    done[...] = dot_tn(act_ref[...], db2_ref[...]).astype(BF)
    keep_ref[0] = done[pl.ds(pl.multiple_of(core * half, 16), half), :]
    send_ref[0] = done[pl.ds(pl.multiple_of((1 - core) * half, 16), half), :]


def grad_outer(at, owners, act, db2):
    rows, hidden = act.shape
    width = db2.shape[1]
    size = hidden // owners
    levels = owners.bit_length() - 1

    def column(i, at_ref):
        mask = 0
        for level in range(levels):
            mask = mask | (((i >> level) & 1) << (levels - 1 - level))
        return (0, at_ref[0] ^ mask)

    out = jax.ShapeDtypeStruct((owners, size // 2, width), BF)
    spec = pl.BlockSpec((1, size // 2, width), lambda i, at_ref: (i, 0, 0))
    return pl.pallas_call(
        lambda *refs: grad_outer_kernel(size // 2, *refs),
        grid_spec=pltpu.PrefetchScalarGridSpec(
            num_scalar_prefetch=1,
            grid=(owners,),
            in_specs=[pl.BlockSpec((rows, size), column), pl.BlockSpec((rows, width), lambda i, at_ref: (0, 0))],
            out_specs=[spec, spec],
            scratch_shapes=[pltpu.VMEM((size, width), BF)],
        ),
        out_shape=[out, out],
        compiler_params=pltpu.CompilerParams(vmem_limit_bytes=LIMIT),
        cost_estimate=pl.CostEstimate(flops=2 * rows * width * hidden, bytes_accessed=4 * rows * hidden, transcendentals=0),
        name="grad_outer",
    )(at, act, db2)


def input_kernel(plan, shard, count, at_ref, dfirst_ref, *rest):
    parts, rest = rest[:count], rest[count:]
    pieces, (out_ref, mat, sems) = rest[:-3], rest[-3:]

    @pl.when(pl.program_id(0) == 0)
    def _():
        for copy in load(qkv_copies(plan, pieces, at_ref, mat, shard), sems):
            copy.wait()

    width = mat.shape[0]
    wide = parts[0].shape[1]
    total = dfirst_ref[...]
    for i, part in enumerate(parts):
        start = (i % 3) * width + (i // 3) * wide
        total = total + dot_nt(part[...], mat[:, start : start + wide])
    out_ref[...] = total.astype(BF)


def input_gradient(at, dfirst, parts, plan, pieces, shard):
    rows, width = dfirst.shape
    blocks = 4
    count = sum(1 if masks is None else len(masks) for masks, _ in plan)

    def row(cols):
        return pl.BlockSpec((rows // blocks, cols), lambda i: (i, 0))

    return pl.pallas_call(
        lambda *refs: input_kernel(plan, shard, len(parts), *refs),
        grid=(blocks,),
        in_specs=[SCALAR, row(width)] + [row(part.shape[1]) for part in parts] + [MAT] * len(pieces),
        out_specs=row(width),
        out_shape=jax.ShapeDtypeStruct((rows, width), BF),
        scratch_shapes=[pltpu.VMEM((width, 3 * width), BF), pltpu.SemaphoreType.DMA((count,))],
        compiler_params=pltpu.CompilerParams(vmem_limit_bytes=LIMIT),
        cost_estimate=pl.CostEstimate(flops=6 * rows * width * width, bytes_accessed=14 * rows * width, transcendentals=0),
        name="input_gradient",
    )(at, dfirst, *parts, *pieces)


def column_sum(value):
    return jnp.sum(value.astype(F32), axis=0)


def fold(parts):
    return sum(part.astype(F32) for part in parts)


def halve(parts):
    half = parts[0].shape[0] // 2
    return fold([part[half:] for part in parts]).astype(BF), [part[:half] for part in parts]


def reduce_to_owner(value, owners):
    index = lax.axis_index("fsdp")
    parts = [value]
    for bit in reversed(bits_of(owners)):
        flag = (index // bit) & 1
        pairs = [part.reshape((-1, 2) + part.shape[1:]) for part in parts]
        sent = fold([pick(flag, pair[:, 1], pair[:, 0]) for pair in pairs]).astype(BF)
        parts = [pick(flag, pair[:, 0], pair[:, 1]) for pair in pairs] + [swap(sent, "fsdp", bit)]
    total = fold([part[0] for part in parts])
    for bit in (1, 2):
        own = total.astype(BF)
        total = own.astype(F32) + swap(own, "seq", bit).astype(F32)
    return total


def body(
    tokens, segment_ids, out_cotangent, query_weight, query_bias, key_weight, value_weight, value_bias,
    output_weight, output_bias, attn_gain, attn_shift, inner_weight, inner_bias, outer_weight, outer_bias,
    final_gain, final_shift,
):
    groups = lax.axis_size("seq")
    owners = lax.axis_size("fsdp")
    micro, seq_count, local_len, width = tokens.shape
    assert micro * seq_count == groups == 4
    rows = groups * local_len
    shard = query_weight.shape[0]
    hidden = inner_weight.shape[1]
    wide = hidden // owners
    lots = wide // shard
    aligned = shard % 32 == 0 and owners == 8
    place = lax.axis_index("seq")
    core = place & 1
    at = jnp.stack([lax.axis_index("fsdp"), place]).astype(jnp.int32)
    masks = order_of(owners)

    def to_sequences(value):
        return lax.all_to_all(value.reshape((groups, local_len) + value.shape[3:]), "seq", 0, 0, tiled=True)

    def to_tokens(value):
        moved = lax.all_to_all(value.reshape(groups, local_len, width), "seq", 0, 0, tiled=True)
        return moved.reshape(micro, seq_count, local_len, width)

    small = jnp.stack(
        [query_bias, value_bias, output_bias, attn_gain, attn_shift, outer_bias, final_gain, final_shift]
        + [inner_bias[i * shard : (i + 1) * shard] for i in range(lots)]
    )
    piece_a = pick(
        core,
        jnp.concatenate([query_weight, key_weight[:, : width // 2]], axis=1),
        jnp.concatenate([key_weight[:, width // 2 :], value_weight], axis=1),
    )
    piece_b = pick(
        core,
        jnp.concatenate([inner_weight[:, : hidden // 2], output_weight[:, : width // 2]], axis=1),
        jnp.concatenate([inner_weight[:, hidden // 2 :], output_weight[:, width // 2 :]], axis=1),
    )
    if aligned:
        index = lax.axis_index("fsdp")

        def join(held, bit):
            other = swap(held, "fsdp", bit)
            flag = (index // bit) & 1
            held = pick(flag, jnp.stack([held, other], axis=1), jnp.stack([other, held], axis=1))
            return held.reshape((-1,) + held.shape[2:])

        a_far = swap(piece_a[None], "fsdp", 4)
        small_far = join(small[None], 4)
        x_rows = to_sequences(tokens).reshape(rows, width)
        doc = to_sequences(segment_ids).reshape(rows, 1)
        a_far, small_far, doc = lax.optimization_barrier((a_far, small_far, doc))
        a_low = jnp.concatenate([piece_a[None], a_far])
        a_two = swap(a_low, "fsdp", 2)
        a_one = swap(a_low, "fsdp", 1)
        small_two = join(small_far, 2)
        a_two, a_one, small_two = lax.optimization_barrier((a_two, a_one, small_two))
        small_full = join(small_two, 1)
        quarter = wide // 4
        piece_c = lax.dynamic_slice(outer_weight, (place * quarter, 0), (quarter, width))[None]
        c_far = swap(after(piece_c, a_two), "fsdp", 4)
        a_three = swap(a_two, "fsdp", 1)
        b_far = swap(after(piece_b, a_two)[None], "fsdp", 4)
        a_mine = [a_low, a_two, a_one, a_three]
        a_other = [swap(value, "seq", 1) for value in a_mine]
        quads = [(0, 4), (2, 6), (1, 5), (3, 7)]
        plan_a = [(quad, 0) for quad in quads] + [(quad, 1) for quad in quads]
        pieces_a = a_mine + a_other
    else:
        small_full = absolute(small[None], owners)
        x_rows = to_sequences(tokens).reshape(rows, width)
        doc = to_sequences(segment_ids).reshape(rows, 1)
        mine = absolute(piece_a[None], owners).reshape(width, -1)
        plan_a = [(None, 0), (None, 1)]
        pieces_a = [mine, swap(mine, "seq", 1)]
    small_full = small_full.astype(F32)
    vecs = small_full[:, :8].transpose(1, 0, 2).reshape(8, width)
    inner_vec = small_full[:, 8:].reshape(1, hidden)
    qkv_vec = jnp.concatenate([vecs[0:1], jnp.zeros((1, width), F32), vecs[1:2]], axis=1)
    ffn_vecs = vecs[2:]

    qkv = project(at, x_rows, qkv_vec, plan_a, pieces_a, shard)
    pairs = width // PAIR
    calls = 3
    each = pairs // calls
    atts, logs = [], []
    if aligned:
        c_low = jnp.concatenate([piece_c, c_far])
        b_low = jnp.concatenate([piece_b[None], b_far])
        qkv, c_low, b_low, gout = lax.optimization_barrier((qkv, c_low, b_low, out_cotangent))
        c_two = swap(c_low, "fsdp", 2)
        c_one = swap(c_low, "fsdp", 1)
        b_two = swap(b_low, "fsdp", 2)
        b_one = swap(b_low, "fsdp", 1)
        att, log = attend(doc, qkv, 0, each)
        atts.append(att)
        logs.append(log)
        grads_in = to_sequences(gout).reshape(rows, width)
        qkv, c_two, c_one, _ = lax.optimization_barrier((qkv, c_two, c_one, att))
        c_three = swap(c_two, "fsdp", 1)
        c_side = [swap(c_low, "seq", 2), swap(c_two, "seq", 2)]
        att, log = attend(doc, qkv, each, each)
        atts.append(att)
        logs.append(log)
        qkv, b_two, b_one, c_three, c_side, grads_in, _ = lax.optimization_barrier(
            (qkv, b_two, b_one, c_three, c_side, grads_in, att)
        )
        c_side = c_side + [swap(c_one, "seq", 2), swap(c_three, "seq", 2)]
        att, log = attend(doc, qkv, 2 * each, each)
        atts.append(att)
        logs.append(log)
        b_three = swap(b_two, "fsdp", 1)
        b_three, b_two, b_one, c_side, _ = lax.optimization_barrier((b_three, b_two, b_one, c_side, att))
        b_mine = [b_low, b_two, b_one, b_three]
        b_other = [swap(value, "seq", 1) for value in b_mine]
        plan_b, pieces_b = plan_a, b_mine + b_other
        c_mine = [c_low, c_two, c_one, c_three]
        c_all = c_mine + c_side
        plan_c = [(quad, mask) for mask in (0, 2, 1, 3) for quad in quads]
        pieces_c = c_all + [swap(value, "seq", 1) for value in c_all]
    else:
        for call in range(calls):
            att, log = attend(doc, qkv, call * each, each)
            atts.append(att)
            logs.append(log)
        grads_in = to_sequences(out_cotangent).reshape(rows, width)
        mine = absolute(piece_b[None], owners).reshape(width, -1)
        plan_b, pieces_b = plan_a, [mine, swap(mine, "seq", 1)]
        plan_c, pieces_c = [(None, 0)], [absolute(outer_weight[None], owners).reshape(hidden, width)]
    result, active, dinner, low, db2, db, dfirst, dattended, sums, dinner_vec = ffn(
        at, x_rows, grads_in, ffn_vecs, inner_vec, atts, plan_b, pieces_b, plan_c, pieces_c, shard
    )
    backs = []

    def back(call, gate):
        return attend_back(doc, qkv, atts[call], gate, logs[call], call * each, each)

    def vectors():
        dq = jnp.concatenate([one[3] for one in backs], axis=1)
        dv = jnp.concatenate([one[4] for one in backs], axis=1)
        eight = jnp.concatenate([dq, dv, sums[:6]]).reshape(8, owners, shard).transpose(1, 0, 2)
        return jnp.concatenate([eight, dinner_vec.reshape(owners, lots, shard)], axis=1)

    if aligned:
        outer_keep, outer_send = grad_outer(at, owners, active, db2)
        outer_parts = [outer_keep, swap(outer_send, "seq", 1)]
        inner_kept, inner_side, inner_core, inner_both = grad_inner(at, masks, after(low, outer_keep), dinner, atts, db)
        outer_x, outer_parts = halve(outer_parts)
        gate = after(dattended, inner_kept, outer_x)
        backs.append(back(0, gate))
        outer_parts.append(swap(outer_x, "fsdp", 1))
        inner_parts = [inner_kept, swap(inner_core, "seq", 1)]
        inner_y = fold([inner_side, swap(inner_both, "seq", 1)]).astype(BF)
        gate, shown, _ = lax.optimization_barrier((gate, result, (backs[0], inner_y, inner_parts)))
        layer_out = to_tokens(shown)
        backs.append(back(1, gate))
        inner_parts.append(swap(inner_y, "seq", 2))
        both = [jnp.concatenate([one[j] for one in backs], axis=1) for j in range(3)]
        first_keep, first_send = grad_wide(at, masks, x_rows, both)
        outer_z, outer_parts = halve(outer_parts)
        gate, layer_out, _ = lax.optimization_barrier((gate, layer_out, (first_keep, outer_z)))
        backs.append(back(2, gate))
        outer_parts.append(swap(outer_z, "fsdp", 2))
        first_parts = [first_keep, swap(first_send, "seq", 1)]
        outer_zz, outer_parts = halve(outer_parts)
        inner_x, inner_parts = halve(inner_parts)
        first_x, first_parts = halve(first_parts)
        extra = vectors()
        extra = jnp.pad(extra, ((0, 0), (0, 16 - extra.shape[1]), (0, each * PAIR - shard))).astype(BF)
        gated, _ = lax.optimization_barrier((x_rows, (outer_zz, inner_x, first_x)))
        second_keep, second_send = grad_wide(at, masks, gated, backs[2][:3], extra)
        dfirst, _ = lax.optimization_barrier((dfirst, (second_keep,)))
        parts = [value for one in backs for value in one[:3]]
        moved = input_gradient(at, dfirst, parts, plan_a, pieces_a, shard)
        input_grad = to_tokens(moved).astype(F32)
        outer_parts.append(swap(outer_zz, "fsdp", 4))
        inner_parts.append(swap(inner_x, "fsdp", 1))
        first_parts.append(swap(first_x, "fsdp", 1))
        second_parts = [second_keep, swap(second_send, "seq", 1)]
        second_x, second_parts = halve(second_parts)
        second_parts.append(swap(second_x, "fsdp", 1))
        groups_left = [inner_parts, first_parts, second_parts]
        for bit in (2, 4):
            sends = [halve(group) for group in groups_left]
            groups_left = [keep + [swap(sent, "fsdp", bit)] for sent, keep in sends]
        owns = [fold([part[0] for part in group]).astype(BF) for group in [outer_parts] + groups_left]
        others = [swap(own, "seq", 2) for own in owns]
        outer_own, first_own, second_own = (
            owns[i].astype(F32) + others[i].astype(F32) for i in (0, 2, 3)
        )
        side = place >> 1
        half = shard // 2
        cols = width // 2
        inner_own = pick(
            side,
            jnp.stack([value.reshape(half, -1, cols) for value in (owns[1], others[1])], axis=2),
            jnp.stack([value.reshape(half, -1, cols) for value in (others[1], owns[1])], axis=2),
        ).reshape(half, hidden + width)

        def whole(own):
            other = swap(own, "seq", 1)
            return pick(core, jnp.concatenate([own, other]), jnp.concatenate([other, own])).astype(F32)

        douter = whole(outer_own)
        dinner_full = whole(inner_own)
        part = 2 * each * PAIR
        firsts = whole(first_own)
        seconds = whole(second_own[:half])
        rest = each * PAIR
        dqkv = [
            jnp.concatenate([firsts[:, i * part : (i + 1) * part], seconds[:, i * rest : (i + 1) * rest]], axis=1)
            for i in range(3)
        ]
        vec = second_own[half : half + 8 + lots, :shard]
        dinner_w, doutput = dinner_full[:, :hidden], dinner_full[:, hidden:]
    else:
        for call in range(calls):
            backs.append(back(call, dattended))
        parts = [value for one in backs for value in one[:3]]
        moved = input_gradient(at, dfirst, parts, plan_a, pieces_a, shard)
        input_grad = to_tokens(moved).astype(F32)
        layer_out = to_tokens(result)
        three = [jnp.concatenate([one[j] for one in backs], axis=1) for j in range(3)]
        att = jnp.concatenate(atts, axis=1)
        lefts = [x_rows, x_rows, x_rows, att, low]
        rights = three + [db, dinner]
        dqkv = []
        for left, right in zip(lefts, rights):
            dqkv.append(reduce_to_owner(dot_tn(left, right).astype(BF).reshape(owners, shard, -1), owners))
        doutput, dinner_w = dqkv[3:]
        douter = reduce_to_owner(dot_tn(active, db2).astype(BF).reshape(owners, wide, width), owners)
        vec = reduce_to_owner(vectors().astype(BF), owners)
    return (
        layer_out, input_grad, dqkv[0], vec[0], dqkv[1], dqkv[2], vec[1], doutput, vec[2], vec[3], vec[4], dinner_w,
        vec[8:].reshape(wide), douter, vec[5], vec[6], vec[7],
    )


def solution(mesh):
    rows = P(None, "fsdp", "seq", None)
    mat = P("fsdp", None)
    vec = P("fsdp")
    return jax.shard_map(
        body,
        mesh=mesh,
        in_specs=(
            rows, P(None, "fsdp", "seq"), rows, mat, vec, mat, mat, vec, mat, vec, vec, vec, mat, vec, mat, vec, vec, vec,
        ),
        out_specs=(rows, rows, mat, vec, mat, mat, vec, mat, vec, vec, vec, mat, vec, mat, vec, vec, vec),
        check_vma=False,
    )
```
